256 devices in a mesh: plate: 8 (over y, x_lo), sub: 32 (over x_hi, z, core).
Axes of the slice: x: 4 (x_hi: 2, x_lo: 2; x = x_hi * 2 + x_lo), y: 4, z: 8, core: 2. Of those that a mesh axis runs over, the one named last changes fastest.
Arguments:
- populations: float32 [19, 32, 512, 128], P(None, 'plate', 'sub'), may hold values from 0.5 to 1.5
- solid: int32 [32, 512, 128], P('plate', 'sub'), may hold values 0 or 1
- marker_corner: int32 [3, 16384], P(None, ('plate', 'sub')), may hold values from 0 to 508, as said below
- marker_frac: float32 [3, 16384], P(None, ('plate', 'sub')), may hold values from 0 to 1
- marker_target: float32 [3, 16384], P(None, ('plate', 'sub')), may hold values from -0.6 to 0.6
- stiffness: float32 [16384], P(('plate', 'sub')), may hold values from 0.5 to 4
- displacement: float32 [3, 16384], P(None, ('plate', 'sub')), may hold values from -0.6 to 0.6
Outputs:
- populations_out: float32 [19, 32, 512, 128], P(None, 'plate', 'sub')
- displacement_out: float32 [3, 16384], P(None, ('plate', 'sub'))
- marker_force: float32 [3, 16384], P(None, ('plate', 'sub'))
The draws below stay inside these ranges and needn't reach their ends.
Inputs may be any that keep to these rules, and one draw needn't show every extreme that they name: `marker_corner`: components are the first cell of the stencil along the three dimensions. Every stencil lies inside the grid without wrapping, and along the first dimension inside the slab of 4 cells that its plate's markers share; the markers of plate p are rows p * 2048 to (p + 1) * 2048 - 1 and lie in slab p.
All inputs are finite; a program needn't handle non-finite values. No bound on the sum of `solid` on one device may be relied on, other than what follows from the above.
Results may differ from the reference program's by a relative error of at most 0.00011.
Values sent between devices are 32-bit elements; how exact they have to be, the bound alone decides.
No kernel may reach another device: no remote copies, remote signals or barrier semaphores. Data moves between devices by JAX's collectives and lax.ppermute only.
A program may use at most 64 MiB of HBM per device.

```python
import math
import jax
import jax.numpy as jnp
from jax import lax

CX = 4
NZ = 128
M_DEV = 64
STEPS = 2
X = 32
Y = 512
MARKERS = 16384
N_PLATE = 8
N_SUB = 32


def draw_marker_corner(key, part):
    per_plate = M_DEV * N_SUB
    total = per_plate * N_PLATE
    y_band = max(Y // 4, 4)
    z_band = max(NZ // 2, 4)
    keys = jax.random.split(key, 5)
    plate_of = jnp.arange(total, dtype=jnp.int32) // per_plate
    y_first = jax.random.randint(keys[0], (N_PLATE,), 0, Y - y_band + 1).astype(jnp.int32)
    z_first = jax.random.randint(keys[1], (N_PLATE,), 0, NZ - z_band + 1).astype(jnp.int32)
    y_first = y_first.at[0].set(0).at[N_PLATE - 1].set(Y - y_band)
    z_first = z_first.at[0].set(0).at[N_PLATE - 1].set(NZ - z_band)
    x_off = jax.random.randint(keys[2], (total,), 0, CX - 3).astype(jnp.int32)
    y_off = jax.random.randint(keys[3], (total,), 0, y_band - 3).astype(jnp.int32)
    z_off = jax.random.randint(keys[4], (total,), 0, z_band - 3).astype(jnp.int32)
    x_off = x_off.at[0].set(0).at[total - 1].set(CX - 4)
    y_off = y_off.at[0].set(0).at[total - 1].set(y_band - 4)
    z_off = z_off.at[0].set(0).at[total - 1].set(z_band - 4)
    x_pos = plate_of * CX + x_off
    y_pos = y_first[plate_of] + y_off
    z_pos = z_first[plate_of] + z_off
    return jnp.stack([x_pos, y_pos, z_pos]).astype(jnp.int32)


def set_ends(entries, key, low, high):
    index_at = [jax.random.randint(jax.random.fold_in(key, axis), (), 0, length) for axis, length in enumerate(entries.shape)]
    widest = entries.shape.index(max(entries.shape))
    next_to = index_at[:widest] + [(index_at[widest] + 1) % entries.shape[widest]] + index_at[widest + 1:]
    return entries.at[tuple(index_at)].set(low).at[tuple(next_to)].set(high)


def block_scale(key, dims, cuts, smallest, top_value):
    level = 1.0
    for position, blocks in cuts:
        heights = jax.random.uniform(jax.random.fold_in(jax.random.fold_in(key, 6), position), (blocks,), jnp.float32, smallest / len(cuts), top_value / len(cuts))
        level = level * jnp.repeat(jnp.exp(heights), dims[position] // blocks).reshape((-1,) + (1,) * (len(dims) - 1 - position))
    return level


def normal_values(key, shape, scale, bound, shards=(), kind=jnp.bfloat16):
    values = scale * jax.random.normal(key, shape, jnp.float32)
    if shards:
        values = values * block_scale(key, shape, shards, -0.22, 0.18)
    return jnp.clip(values, -bound, bound).astype(kind)


def setup_inputs(seed: int = 0) -> dict:
    splits = jax.random.split(jax.random.key(seed), 8)
    return {
        "populations": jnp.clip(0.5 + 1.0 * jax.random.uniform(splits[0], (19, X, Y, NZ), jnp.float32) ** block_scale(splits[0], (19, X, Y, NZ), ((1, 8), (2, 32)), -0.2, 0.2), 0.5, 1.5),
        "solid": set_ends((jax.random.randint(splits[1], (X, Y, NZ), 0, 8) < 1).astype(jnp.int32), jax.random.fold_in(splits[1], 1), 0, 1),
        "marker_corner": draw_marker_corner(jax.random.fold_in(splits[7], 71), 0),
        "marker_frac": jnp.clip(1.0 * jax.random.uniform(splits[3], (3, MARKERS), jnp.float32) ** block_scale(splits[3], (3, MARKERS), ((1, 256),), -0.2, 0.2), 0.0, 1.0),
        "marker_target": normal_values(splits[4], (3, MARKERS), 0.1, 0.6, ((1, 256),), jnp.float32),
        "stiffness": jnp.clip(jnp.exp(math.log(4.0) - 2.0794415 * jax.random.uniform(splits[5], (MARKERS,), jnp.float32) ** block_scale(splits[5], (MARKERS,), ((0, 256),), -0.2, 0.2)), 0.5, 4.0),
        "displacement": normal_values(splits[6], (3, MARKERS), 0.1, 0.6, ((1, 256),), jnp.float32),
    }


DIRS = [(0, 0, 0), (1, 0, 0), (-1, 0, 0), (0, 1, 0), (0, -1, 0), (0, 0, 1), (0, 0, -1), (1, 1, 0), (-1, -1, 0), (1, -1, 0), (-1, 1, 0), (1, 0, 1), (-1, 0, -1), (1, 0, -1), (-1, 0, 1), (0, 1, 1), (0, -1, -1), (0, 1, -1), (0, -1, 1)]
WEIGHTS = [1.0 / 3.0] + [1.0 / 18.0] * 6 + [1.0 / 36.0] * 12
OPPOSITE = [0, 2, 1, 4, 3, 6, 5, 8, 7, 10, 9, 12, 11, 14, 13, 16, 15, 18, 17]
KAPPA = 4.0
RELAX = 0.9

def kernel_weights(frac):
    root = jnp.sqrt(1.0 + 4.0 * frac - 4.0 * frac * frac)
    second = (3.0 - 2.0 * frac + root) / 8.0
    third = (1.0 + 2.0 * frac + root) / 8.0
    return jnp.stack([0.5 - third, second, third, 0.5 - second])

def moments(pops):
    density = lax.optimization_barrier(jnp.sum(pops, 0))
    comps = []
    for axis in range(3):
        total = jnp.zeros_like(density)
        for index in range(19):
            if DIRS[index][axis] == 1:
                total = total + pops[index]
            elif DIRS[index][axis] == -1:
                total = total - pops[index]
        comps.append(total)
    return (density, jnp.stack(comps) / density)

def dotted(index, vectors):
    total = jnp.zeros_like(vectors[0])
    for axis in range(3):
        if DIRS[index][axis] == 1:
            total = total + vectors[axis]
        elif DIRS[index][axis] == -1:
            total = total - vectors[axis]
    return total

def collide(pops, density, velocity, spread, fluid):
    speed_sq = lax.optimization_barrier(jnp.sum(velocity * velocity, 0))
    result = []
    for index in range(19):
        proj = dotted(index, velocity)
        equil = WEIGHTS[index] * density * (1.0 + 3.0 * proj + 4.5 * proj * proj - 1.5 * speed_sq)
        post = pops[index] - (pops[index] - equil) / RELAX + 3.0 * WEIGHTS[index] * dotted(index, spread)
        result.append(jnp.where(fluid, post, pops[OPPOSITE[index]]))
    return jnp.stack(result)

def reference(populations, solid, marker_corner, marker_frac, marker_target, stiffness, displacement):
    x_weights = kernel_weights(marker_frac[0])
    y_weights = kernel_weights(marker_frac[1])
    z_weights = kernel_weights(marker_frac[2])
    fluid = solid == 0
    disp = displacement
    force = jnp.zeros_like(displacement)
    pops = populations
    for step in range(STEPS):
        density, velocity = moments(pops)
        marker_vel = jnp.zeros_like(displacement)
        for dx in range(4):
            for dy in range(4):
                for dz in range(4):
                    factor = x_weights[dx] * y_weights[dy] * z_weights[dz]
                    picked = velocity[:, marker_corner[0] + dx, marker_corner[1] + dy, marker_corner[2] + dz]
                    marker_vel = marker_vel + factor[None] * picked
        force = KAPPA * (marker_target - marker_vel) - stiffness[None] * disp
        disp = disp + marker_vel
        spread = jnp.zeros_like(velocity)
        for dx in range(4):
            for dy in range(4):
                for dz in range(4):
                    factor = x_weights[dx] * y_weights[dy] * z_weights[dz]
                    spread = spread.at[:, marker_corner[0] + dx, marker_corner[1] + dy, marker_corner[2] + dz].add(factor[None] * force)
        post = collide(pops, density, velocity, spread, fluid)
        pops = jnp.stack([jnp.roll(post[index], DIRS[index], axis=(0, 1, 2)) for index in range(19)])
    return (pops, disp, force)
```

```python
import functools
import jax
import jax.numpy as jnp
from jax import lax
from jax.experimental import pallas as pl
from jax.experimental.pallas import tpu as pltpu
from jax.sharding import PartitionSpec as P

DIRS = [
    (0, 0, 0),
    (1, 0, 0),
    (-1, 0, 0),
    (0, 1, 0),
    (0, -1, 0),
    (0, 0, 1),
    (0, 0, -1),
    (1, 1, 0),
    (-1, -1, 0),
    (1, -1, 0),
    (-1, 1, 0),
    (1, 0, 1),
    (-1, 0, -1),
    (1, 0, -1),
    (-1, 0, 1),
    (0, 1, 1),
    (0, -1, -1),
    (0, 1, -1),
    (0, -1, 1),
]
WEIGHTS = [1.0 / 3.0] + [1.0 / 18.0] * 6 + [1.0 / 36.0] * 12
KAPPA = 4.0
RELAX = 0.9
UP = [i for i in range(19) if DIRS[i][0] == 1]
DOWN = [i for i in range(19) if DIRS[i][0] == -1]

CX = 4
ROWS = 16
HALO = 8
EXT = ROWS + 2 * HALO
NZ = 128
XY = CX * EXT
LANES = 128
F32 = jnp.float32
BF16 = jnp.bfloat16


def split(value):
    high = value.astype(BF16)
    low = (value - high.astype(F32)).astype(BF16)
    return high, low


def moments_of(pop):
    values = [pop(i) for i in range(19)]
    density = functools.reduce(lambda a, b: a + b, values)
    inverse = 1.0 / density
    velocity = []
    for axis in range(3):
        plus = functools.reduce(lambda a, b: a + b, [values[i] for i in range(19) if DIRS[i][axis] == 1])
        minus = functools.reduce(lambda a, b: a + b, [values[i] for i in range(19) if DIRS[i][axis] == -1])
        velocity.append((plus - minus) * inverse)
    return density, velocity


def along(index, vectors):
    total = None
    for axis in range(3):
        sign = DIRS[index][axis]
        if sign == 0:
            continue
        if total is None:
            total = vectors[axis] if sign == 1 else -vectors[axis]
        else:
            total = total + vectors[axis] if sign == 1 else total - vectors[axis]
    return total


def collide(pop, density, velocity, force, solid, put):
    keep, rate = 1.0 - 1.0 / RELAX, 1.0 / RELAX
    scaled = density * rate
    base = scaled - 1.5 * scaled * (
        velocity[0] * velocity[0] + velocity[1] * velocity[1] + velocity[2] * velocity[2]
    )
    rest = pop(0)
    put(0, jnp.where(solid, rest, keep * rest + WEIGHTS[0] * base))
    for index in range(1, 19, 2):
        weight = WEIGHTS[index]
        first, second = pop(index), pop(index + 1)
        proj = along(index, velocity)
        scaled_proj = scaled * proj
        even = weight * (base + 4.5 * scaled_proj * proj)
        odd = (3.0 * weight) * (scaled_proj + along(index, force))
        put(index, jnp.where(solid, second, keep * first + (even + odd)))
        put(index + 1, jnp.where(solid, first, keep * second + (even - odd)))


def interpolate_and_spread(vcat, zcat, xy, state, weighted, spread, new_state):
    for tile in range(8):
        cols = slice(tile * 256, (tile + 1) * 256)
        z_high, z_low = zcat[0:128, cols], zcat[128:256, cols]
        found = jnp.dot(vcat[...], jnp.concatenate([z_high, z_high], 0), preferred_element_type=F32)
        found = found + jnp.dot(vcat[:, 0:128], z_low, preferred_element_type=F32)
        planes = xy[:, cols]
        for axis in range(3):
            mean = jnp.sum(found[axis * XY : (axis + 1) * XY] * planes, axis=0, keepdims=True)
            disp = state[4 + axis : 5 + axis, cols]
            force = KAPPA * (state[axis : axis + 1, cols] - mean) - state[3:4, cols] * disp
            new_state(axis, cols, disp + mean, force)
            high, low = split(planes * force)
            weighted[axis * XY : (axis + 1) * XY, cols] = high
            weighted[(3 + axis) * XY : (4 + axis) * XY, cols] = low
    spread[...] = lax.dot_general(
        weighted[...], zcat[...], (((1,), (1,)), ((), ())), preferred_element_type=F32
    )


def spread_at(spread, x, row, rows):
    result = []
    for axis in range(3):
        at = axis * XY + x * EXT + row
        result.append(
            spread[at : at + rows, 0:128]
            + spread[at : at + rows, 128:256]
            + spread[3 * XY + at : 3 * XY + at + rows, 0:128]
        )
    return result


def moved(block, index):
    _, shift_y, shift_z = DIRS[index]
    if shift_y:
        block = pltpu.roll(block, shift_y % block.shape[0], 0)
    if shift_z:
        block = pltpu.roll(block, shift_z % NZ, 1)
    return block


def first_kernel(
    own, low, high, solid, markers, part, up, down, zcat, xy, state, vcat, weighted, spread, rho, vel, post
):
    for x in range(CX):
        for half in range(2):

            def pop(i):
                if half == 0:
                    return jnp.concatenate([low[i, x], own[i, x, 0:8]], 0)
                return jnp.concatenate([own[i, x, 8:16], high[i, x]], 0)

            density, velocity = moments_of(pop)
            rows = slice(half * 16, half * 16 + 16)
            rho[x, rows] = density
            for axis in range(3):
                vel[axis, x, rows] = velocity[axis]
                at = axis * XY + x * EXT + half * 16
                vcat[at : at + 16, 0:128], vcat[at : at + 16, 128:256] = split(velocity[axis])

    left = lax.broadcasted_iota(jnp.int32, (6, LANES), 1) < 64
    z_cell = lax.broadcasted_iota(jnp.int32, (NZ, LANES), 0).astype(F32)
    y_cell = lax.broadcasted_iota(jnp.int32, (EXT, LANES), 0).astype(F32) - HALO
    for tile in range(16):
        cols = slice(tile * LANES, (tile + 1) * LANES)
        one, two = markers[2 * tile], markers[2 * tile + 1]
        even = jnp.where(left, one, pltpu.roll(two, 64, 1))
        odd = jnp.where(left, pltpu.roll(one, 64, 1), two)

        def kernel_weights(frac):
            root = jnp.sqrt(1.0 + 4.0 * frac - 4.0 * frac * frac)
            second = (3.0 - 2.0 * frac + root) / 8.0
            third = (1.0 + 2.0 * frac + root) / 8.0
            return [0.5 - third, second, third, 0.5 - second]

        def dense(cells, first, weights):
            offset = cells - first
            value = jnp.where(offset == 3.0, weights[3], 0.0)
            for k in (2, 1, 0):
                value = jnp.where(offset == float(k), weights[k], value)
            return value

        kx, ky, kz = kernel_weights(even[1:2]), kernel_weights(odd[1:2]), kernel_weights(even[2:3])
        zcat[0:128, cols], zcat[128:256, cols] = split(dense(z_cell, odd[0:1], kz))
        y_rows = dense(y_cell, even[0:1], ky)
        for x in range(CX):
            xy[x * EXT : (x + 1) * EXT, cols] = kx[x] * y_rows
        rows = (even[3:4], odd[3:4], even[4:5], odd[2:3], odd[4:5], even[5:6], odd[5:6], even[0:1])
        for r, value in enumerate(rows):
            state[r : r + 1, cols] = value

    def new_state(axis, cols, disp, force):
        state[4 + axis : 5 + axis, cols] = disp

    interpolate_and_spread(vcat, zcat, xy, state, weighted, spread, new_state)

    for x in range(CX):
        for tile in range(4):
            rows = slice(tile * 8, tile * 8 + 8)

            def pop(i):
                if tile == 0:
                    return low[i, x]
                if tile == 3:
                    return high[i, x]
                return own[i, x, tile * 8 - 8 : tile * 8]

            def put(i, value):
                post[i, x, rows] = value

            if tile == 0:
                wall = low[19, x] != 0.0
            elif tile == 3:
                wall = high[19, x] != 0.0
            else:
                wall = solid[x, tile * 8 - 8 : tile * 8] != 0
            collide(
                pop,
                rho[x, rows],
                [vel[axis, x, rows] for axis in range(3)],
                spread_at(spread, x, tile * 8, 8),
                wall,
                put,
            )
    for index in range(19):
        for x in range(CX):
            source = x - DIRS[index][0]
            if 0 <= source < CX:
                part[index, x] = moved(post[index, source], index)
    for j, index in enumerate(UP):
        up[j] = moved(post[index, CX - 1], index)
    for j, index in enumerate(DOWN):
        down[j] = moved(post[index, 0], index)


def second_kernel(
    part, up, down, low, high, solid, zcat, xy, state, out, out_up, out_down, back,
    vcat, weighted, spread, rho, vel, post, result
):
    def value_of(i, x, rows):
        if x == 0 and DIRS[i][0] == 1:
            return up[UP.index(i), rows]
        if x == CX - 1 and DIRS[i][0] == -1:
            return down[DOWN.index(i), rows]
        return part[i, x, rows]

    row = lax.broadcasted_iota(jnp.int32, (16, NZ), 0)
    for x in range(CX):
        for half in range(2):
            rows = slice(half * 16, half * 16 + 16)
            density, velocity = moments_of(lambda i: value_of(i, x, rows))
            rho[x, rows] = density
            valid = row >= 4 if half == 0 else row < 12
            for axis in range(3):
                known = jnp.where(valid, velocity[axis], 0.0)
                vel[axis, x, rows] = known
                at = axis * XY + x * EXT + half * 16
                vcat[at : at + 16, 0:128], vcat[at : at + 16, 128:256] = split(known)

    def new_state(axis, cols, disp, force):
        result[axis : axis + 1, cols] = disp
        result[3 + axis : 4 + axis, cols] = force

    interpolate_and_spread(vcat, zcat, xy, state, weighted, spread, new_state)

    left = lax.broadcasted_iota(jnp.int32, (1, LANES), 1) < 64
    for tile in range(16):
        cols = slice(tile * LANES, (tile + 1) * LANES)
        first = state[7:8, cols]
        mine = (first >= 0.0) & (first < float(ROWS))
        values = [jnp.where(mine, result[r : r + 1, cols], 0.0) for r in range(6)]
        for r in range(3):
            even, odd = values[2 * r], values[2 * r + 1]
            back[2 * tile, r : r + 1] = jnp.where(left, even, pltpu.roll(odd, 64, 1))
            back[2 * tile + 1, r : r + 1] = jnp.where(left, pltpu.roll(even, 64, 1), odd)

    for x in range(CX):
        for tile in range(4):
            rows = slice(tile * 8, tile * 8 + 8)

            def put(i, value):
                post[i, x, rows] = value

            if tile == 0:
                wall = low[19, x] != 0.0
            elif tile == 3:
                wall = high[19, x] != 0.0
            else:
                wall = solid[x, tile * 8 - 8 : tile * 8] != 0
            collide(
                lambda i: value_of(i, x, rows),
                rho[x, rows],
                [vel[axis, x, rows] for axis in range(3)],
                spread_at(spread, x, tile * 8, 8),
                wall,
                put,
            )

    def inner(index, source):
        return moved(post[index, source], index)[HALO : HALO + ROWS]

    for index in range(19):
        for x in range(CX):
            source = x - DIRS[index][0]
            if 0 <= source < CX:
                out[index, x] = inner(index, source)
    for j, index in enumerate(UP):
        out_up[j] = inner(index, CX - 1)
        out[index, 0] = jnp.zeros((ROWS, NZ), F32)
    for j, index in enumerate(DOWN):
        out_down[j] = inner(index, 0)
        out[index, CX - 1] = jnp.zeros((ROWS, NZ), F32)


def fill_kernel(part, up, down, out, sems):
    copies = []
    for j, index in enumerate(UP):
        copies.append(pltpu.make_async_copy(up.at[j], out.at[index, 0], sems.at[j]))
    for j, index in enumerate(DOWN):
        copies.append(pltpu.make_async_copy(down.at[j], out.at[index, CX - 1], sems.at[5 + j]))
    for copy in copies:
        copy.start()
    for copy in copies:
        copy.wait()


def shape(*dims, dtype=F32):
    return jax.ShapeDtypeStruct(dims, dtype)


WORK = [
    pltpu.VMEM((3 * XY, 2 * NZ), BF16),
    pltpu.VMEM((6 * XY, 2048), BF16),
    pltpu.VMEM((6 * XY, 2 * NZ), F32),
    pltpu.VMEM((CX, EXT, NZ), F32),
    pltpu.VMEM((3, CX, EXT, NZ), F32),
    pltpu.VMEM((19, CX, EXT, NZ), F32),
]
IN_VMEM = pl.BlockSpec(memory_space=pltpu.VMEM)
ANYWHERE = pl.BlockSpec(memory_space=pl.ANY)


def ring(axis):
    peers = lax.axis_size(axis)
    forward = [(i, (i + 1) % peers) for i in range(peers)]
    return forward, [(j, i) for i, j in forward]


def shards(populations, solid, marker_corner, marker_frac, marker_target, stiffness, displacement):
    peers = lax.axis_size("sub")
    block = jnp.concatenate(
        [
            marker_corner[1:].astype(F32),
            marker_frac,
            stiffness[None],
            marker_target,
            displacement,
        ]
    ).reshape(6, LANES)
    at_row = lax.broadcasted_iota(jnp.int32, (peers, 6, LANES), 1)
    at_lane = lax.broadcasted_iota(jnp.int32, (peers, 6, LANES), 2)
    start = lax.broadcasted_iota(jnp.int32, (peers, 6, LANES), 0) * ROWS
    period = float(peers * ROWS)
    first = block[None] - start.astype(F32)
    first = first - jnp.where(first >= period / 2, period, jnp.where(first < -period / 2, -period, 0.0))
    sent = jnp.where((at_row == 0) & (at_lane < 64), first, block[None])
    markers = lax.all_to_all(sent, "sub", 0, 0, tiled=True)

    sub_up, sub_down = ring("sub")
    plate_up, plate_down = ring("plate")
    walls = solid.astype(F32)[None]
    tall = jnp.concatenate([populations, walls], 0)
    low = lax.ppermute(tall[:, :, ROWS - HALO :], "sub", sub_up)
    high = lax.ppermute(tall[:, :, :HALO], "sub", sub_down)

    part, up, down, zcat, xy, state = pl.pallas_call(
        first_kernel,
        out_shape=(
            shape(19, CX, EXT, NZ),
            shape(5, EXT, NZ),
            shape(5, EXT, NZ),
            shape(2 * NZ, 2048, dtype=BF16),
            shape(XY, 2048),
            shape(8, 2048),
        ),
        in_specs=[IN_VMEM] * 5,
        out_specs=[IN_VMEM] * 6,
        scratch_shapes=WORK,
        name="first",
    )(populations, low, high, solid, markers)
    up = lax.ppermute(up, "plate", plate_up)
    down = lax.ppermute(down, "plate", plate_down)
    part, up, down, back = pl.pallas_call(
        second_kernel,
        out_shape=(
            shape(19, CX, ROWS, NZ),
            shape(5, ROWS, NZ),
            shape(5, ROWS, NZ),
            shape(peers, 3, LANES),
        ),
        in_specs=[IN_VMEM] * 9,
        out_specs=[IN_VMEM] * 4,
        scratch_shapes=[*WORK, pltpu.VMEM((8, 2048), F32)],
        name="second",
    )(part, up, down, low, high, solid, zcat, xy, state)
    up = lax.ppermute(up, "plate", plate_up)
    down = lax.ppermute(down, "plate", plate_down)
    result = jnp.sum(lax.all_to_all(back, "sub", 0, 0, tiled=True), 0).reshape(6, 64)
    out = pl.pallas_call(
        fill_kernel,
        out_shape=shape(19, CX, ROWS, NZ),
        in_specs=[ANYWHERE] * 3,
        out_specs=ANYWHERE,
        scratch_shapes=[pltpu.SemaphoreType.DMA((10,))],
        input_output_aliases={0: 0},
        name="fill",
    )(part, up, down)
    return (out, result[:3], result[3:])


def solution(mesh):
    in_specs = (
        P(None, "plate", "sub", None),
        P("plate", "sub", None),
        P(None, ("plate", "sub")),
        P(None, ("plate", "sub")),
        P(None, ("plate", "sub")),
        P(("plate", "sub")),
        P(None, ("plate", "sub")),
    )
    out_specs = (
        P(None, "plate", "sub", None),
        P(None, ("plate", "sub")),
        P(None, ("plate", "sub")),
    )
    return jax.shard_map(shards, mesh=mesh, in_specs=in_specs, out_specs=out_specs, check_vma=False)
```

```python
import functools
import jax
import jax.numpy as jnp
from jax import lax
from jax.experimental import pallas as pl
from jax.experimental.pallas import tpu as pltpu
from jax.sharding import PartitionSpec as P

DIRS = [
    (0, 0, 0),
    (1, 0, 0),
    (-1, 0, 0),
    (0, 1, 0),
    (0, -1, 0),
    (0, 0, 1),
    (0, 0, -1),
    (1, 1, 0),
    (-1, -1, 0),
    (1, -1, 0),
    (-1, 1, 0),
    (1, 0, 1),
    (-1, 0, -1),
    (1, 0, -1),
    (-1, 0, 1),
    (0, 1, 1),
    (0, -1, -1),
    (0, 1, -1),
    (0, -1, 1),
]
WEIGHTS = [1.0 / 3.0] + [1.0 / 18.0] * 6 + [1.0 / 36.0] * 12
KAPPA = 4.0
RELAX = 0.9
UP = [i for i in range(19) if DIRS[i][0] == 1]
DOWN = [i for i in range(19) if DIRS[i][0] == -1]

CX = 4
ROWS = 16
HALO = 8
EXT = ROWS + 2 * HALO
NZ = 128
XY = CX * EXT
TRIM = 4
INNER = EXT - 2 * TRIM
MARKERS = 2048
INSIDE, OUTSIDE = (1, 2), (0, 3)
LANES = 128
F32 = jnp.float32
BF16 = jnp.bfloat16


def split(value):
    high = value.astype(BF16)
    low = (value - high.astype(F32)).astype(BF16)
    return high, low


def moments_of(values):
    density = functools.reduce(lambda a, b: a + b, values)
    inverse = 1.0 / density
    velocity = []
    for axis in range(3):
        plus = functools.reduce(lambda a, b: a + b, [values[i] for i in range(19) if DIRS[i][axis] == 1])
        minus = functools.reduce(lambda a, b: a + b, [values[i] for i in range(19) if DIRS[i][axis] == -1])
        velocity.append((plus - minus) * inverse)
    return density, velocity


def along(index, vectors):
    total = None
    for axis in range(3):
        sign = DIRS[index][axis]
        if sign == 0:
            continue
        if total is None:
            total = vectors[axis] if sign == 1 else -vectors[axis]
        else:
            total = total + vectors[axis] if sign == 1 else total - vectors[axis]
    return total


def relaxed(values, density, velocity, fluid, put):
    keep, rate = 1.0 - 1.0 / RELAX, 1.0 / RELAX
    scaled = density * rate
    base = scaled - 1.5 * scaled * (
        velocity[0] * velocity[0] + velocity[1] * velocity[1] + velocity[2] * velocity[2]
    )
    put(0, jnp.where(fluid, keep * values[0] + WEIGHTS[0] * base, values[0]))
    for index in range(1, 19, 2):
        weight = WEIGHTS[index]
        first, second = values[index], values[index + 1]
        proj = along(index, velocity)
        scaled_proj = scaled * proj
        even = weight * (base + 4.5 * scaled_proj * proj)
        odd = (3.0 * weight) * scaled_proj
        put(index, jnp.where(fluid, keep * first + (even + odd), second))
        put(index + 1, jnp.where(fluid, keep * second + (even - odd), first))


def forced(base, force, put):
    put(0, base(0))
    for index in range(1, 19, 2):
        push = (3.0 * WEIGHTS[index]) * along(index, force)
        put(index, base(index) + push)
        put(index + 1, base(index + 1) - push)


def interpolated(velocity, zcat, planes, cols, rows):
    z_high, z_low = zcat[0:NZ, cols], zcat[NZ : 2 * NZ, cols]
    found = jnp.dot(velocity, jnp.concatenate([z_high, z_high], 0), preferred_element_type=F32)
    found = found + jnp.dot(velocity[:, 0:NZ], z_low, preferred_element_type=F32)
    return [
        jnp.sum(found[axis * rows : (axis + 1) * rows] * planes, axis=0, keepdims=True) for axis in range(3)
    ]


def weigh(weighted, planes, forces, cols, rows):
    for axis in range(3):
        high, low = split(planes * forces[axis])
        weighted[axis * rows : (axis + 1) * rows, cols] = high
        weighted[(3 + axis) * rows : (4 + axis) * rows, cols] = low


def contract(weighted, zcat):
    return lax.dot_general(weighted, zcat, (((1,), (1,)), ((), ())), preferred_element_type=F32)


def spread_at(spread, at, rows, total, fluid):
    result = []
    for axis in range(3):
        high, low = axis * total + at, (3 + axis) * total + at
        whole = spread[high : high + rows, 0:NZ] + spread[high : high + rows, NZ : 2 * NZ]
        result.append((whole + spread[low : low + rows, 0:NZ]) * fluid)
    return result


def moved(block, index, offset):
    _, shift_y, shift_z = DIRS[index]
    shift_y = (shift_y - offset) % block.shape[0]
    if shift_y:
        block = pltpu.roll(block, shift_y, 0)
    if shift_z:
        block = pltpu.roll(block, shift_z % NZ, 1)
    return block


def pack_kernel(own, solid, corner, frac, target, stiffness, disp, sent, bottom, top, block, walls, *held):
    sems = held[-1]
    held = held[:-1]
    small = [
        pltpu.make_async_copy(source, target_ref, sems.at[k])
        for k, (source, target_ref) in enumerate(zip((corner, frac, target, stiffness, disp), held))
    ]
    large = [
        pltpu.make_async_copy(solid, walls, sems.at[5]),
        pltpu.make_async_copy(own.at[:, :, ROWS - HALO :], bottom.at[0:19], sems.at[6]),
        pltpu.make_async_copy(own.at[:, :, :HALO], top.at[0:19], sems.at[7]),
    ]
    for copy in small + large:
        copy.start()
    for copy in small:
        copy.wait()
    corner, frac, target, stiffness, disp = held
    values = [corner[1:2].astype(F32), corner[2:3].astype(F32), frac[0:1], frac[1:2], frac[2:3], stiffness[...]]
    values += [target[axis : axis + 1] for axis in range(3)] + [disp[axis : axis + 1] for axis in range(3)]
    for r, value in enumerate(values):
        block[r // 2 : r // 2 + 1, 64 * (r % 2) : 64 * (r % 2) + 64] = value
    whole = block[0:6]
    peers = sent.shape[0]
    period = float(peers * ROWS)
    first = (lax.broadcasted_iota(jnp.int32, (6, LANES), 0) == 0) & (
        lax.broadcasted_iota(jnp.int32, (6, LANES), 1) < 64
    )
    for peer in range(peers):
        away = whole - float(peer * ROWS)
        away = away - jnp.where(away >= period / 2, period, jnp.where(away < -period / 2, -period, 0.0))
        sent[peer] = jnp.where(first, away, whole)
    for copy in large:
        copy.wait()
    for x in range(CX):
        wall = walls[x].astype(F32)
        bottom[19, x], top[19, x] = wall[ROWS - HALO :], wall[:HALO]


def relax_kernel(low, top, bottom, high, vcat, base, fluid, fluid_inner):
    for x in range(CX):
        wall = jnp.concatenate([part[19, x] for part in (low, top, bottom, high)], 0)
        is_fluid = 1.0 - wall
        fluid[x] = is_fluid
        fluid_inner[x] = pltpu.roll(is_fluid, EXT - TRIM, 0)[0:INNER]
        for half in range(2):
            rows = slice(half * 16, half * 16 + 16)

            def pop(i):
                before, after = (low, top) if half == 0 else (bottom, high)
                return jnp.concatenate([before[i, x], after[i, x]], 0)

            values = [pop(i) for i in range(19)]
            density, velocity = moments_of(values)
            for axis in range(3):
                at = axis * XY + x * EXT + half * 16
                vcat[at : at + 16, 0:NZ], vcat[at : at + 16, NZ : 2 * NZ] = split(velocity[axis])

            def put(i, value):
                base[i, x, rows] = value

            relaxed(values, density, velocity, is_fluid[rows] > 0.5, put)


def dense(cells, first, weights):
    offset = cells - first
    value = jnp.where(offset == 3.0, weights[3], 0.0)
    for k in (2, 1, 0):
        value = jnp.where(offset == float(k), weights[k], value)
    return value


def kernel_weights(frac):
    root = jnp.sqrt(1.0 + 4.0 * frac - 4.0 * frac * frac)
    second = (3.0 - 2.0 * frac + root) / 8.0
    third = (1.0 + 2.0 * frac + root) / 8.0
    return [0.5 - third, second, third, 0.5 - second]


def first_kernel(markers, vcat, base, fluid, post, up, down, zcat, state, xy, weighted, spread):
    left = lax.broadcasted_iota(jnp.int32, (6, LANES), 1) < 64
    z_cell = lax.broadcasted_iota(jnp.int32, (NZ, LANES), 0).astype(F32)
    y_cell = lax.broadcasted_iota(jnp.int32, (EXT, LANES), 0).astype(F32) - HALO
    for tile in range(16):
        cols = slice(tile * LANES, (tile + 1) * LANES)
        one, two = markers[2 * tile], markers[2 * tile + 1]
        even = jnp.where(left, one, pltpu.roll(two, 64, 1))
        odd = jnp.where(left, pltpu.roll(one, 64, 1), two)
        kx, ky, kz = kernel_weights(even[1:2]), kernel_weights(odd[1:2]), kernel_weights(even[2:3])
        zcat[0:NZ, cols], zcat[NZ : 2 * NZ, cols] = split(dense(z_cell, odd[0:1], kz))
        y_rows = dense(y_cell, even[0:1], ky)
        for x in range(CX):
            xy[x * EXT : (x + 1) * EXT, cols] = kx[x] * y_rows
        rows = (even[3:4], odd[3:4], even[4:5], odd[2:3], odd[4:5], even[5:6], odd[5:6], even[0:1], *kx, *ky)
        for r, value in enumerate(rows):
            state[r : r + 1, cols] = value

    for tile in range(8):
        cols = slice(tile * 256, (tile + 1) * 256)
        planes = xy[:, cols]
        forces = []
        for axis, mean in enumerate(interpolated(vcat[...], zcat, planes, cols, XY)):
            disp = state[4 + axis : 5 + axis, cols]
            forces.append(KAPPA * (state[axis : axis + 1, cols] - mean) - state[3:4, cols] * disp)
            state[4 + axis : 5 + axis, cols] = disp + mean
        weigh(weighted, planes, forces, cols, XY)
    spread[...] = contract(weighted[...], zcat[...])

    for x in range(CX):
        for tile in range(4):
            rows = slice(tile * 8, tile * 8 + 8)

            def put(i, value):
                post[i, x, rows] = value

            force = spread_at(spread, x * EXT + tile * 8, 8, XY, fluid[x, rows])
            forced(lambda i: base[i, x, rows], force, put)
    for j, index in enumerate(UP):
        up[j] = moved(post[index, CX - 1], index, TRIM)[0:INNER]
    for j, index in enumerate(DOWN):
        down[j] = moved(post[index, 0], index, TRIM)[0:INNER]


def relax_planes(plane_values, planes, fluid, base, velocities):
    for p, x in enumerate(planes):
        for tile in range(3):
            rows = slice(tile * 8, tile * 8 + 8)
            values = plane_values(x, rows)
            density, velocity = moments_of(values)
            for axis in range(3):
                at = (axis * 2 + p) * INNER + tile * 8
                velocities[at : at + 8, 0:NZ] = velocity[axis]

            def put(i, value):
                base[i, p, rows] = value

            relaxed(values, density, velocity, fluid[x, rows] > 0.5, put)


def inner_kernel(post, fluid, state, zcat, edge, base, found, xy, moving, velocities):
    for index in range(19):
        for x in range(CX):
            source = x - DIRS[index][0]
            if not 0 <= source < CX:
                continue
            plane = moved(post[index, source], index, TRIM)[0:INNER]
            if x in INSIDE:
                moving[index, x - 1] = plane
            else:
                edge[index, x // 3] = plane
    relax_planes(
        lambda x, rows: [moving[i, x - 1, rows] for i in range(19)], INSIDE, fluid, base, velocities
    )
    velocity = jnp.concatenate(split(velocities[...]), 1)
    y_cell = lax.broadcasted_iota(jnp.int32, (INNER, 256), 0).astype(F32) - (HALO - TRIM)
    for tile in range(8):
        cols = slice(tile * 256, (tile + 1) * 256)
        y_rows = dense(y_cell, state[7:8, cols], [state[12 + k : 13 + k, cols] for k in range(4)])
        for p, x in enumerate(INSIDE + OUTSIDE):
            xy[p * INNER : (p + 1) * INNER, cols] = state[8 + x : 9 + x, cols] * y_rows
        parts = interpolated(velocity, zcat, xy[0 : 2 * INNER, cols], cols, 2 * INNER)
        for axis in range(3):
            found[axis : axis + 1, cols] = parts[axis]


def second_kernel(edge, up, down, fluid, state, zcat, xy, found, base, force, back, velocities, moved_to):
    def plane_values(x, rows):
        def value(i):
            if x == 0 and DIRS[i][0] == 1:
                return up[UP.index(i), rows]
            if x == CX - 1 and DIRS[i][0] == -1:
                return down[DOWN.index(i), rows]
            return edge[i, x // 3, rows]

        return [value(i) for i in range(19)]

    relax_planes(plane_values, OUTSIDE, fluid, base, velocities)
    velocity = jnp.concatenate(split(velocities[...]), 1)
    left = lax.broadcasted_iota(jnp.int32, (1, LANES), 1) < 64
    for tile in range(8):
        cols = slice(tile * 256, (tile + 1) * 256)
        parts = interpolated(velocity, zcat, xy[2 * INNER : 4 * INNER, cols], cols, 2 * INNER)
        first = state[7:8, cols]
        mine = (first >= 0.0) & (first < float(ROWS))
        for axis in range(3):
            mean = found[axis : axis + 1, cols] + parts[axis]
            disp = state[4 + axis : 5 + axis, cols]
            pull = KAPPA * (state[axis : axis + 1, cols] - mean) - state[3:4, cols] * disp
            force[axis : axis + 1, cols] = pull
            moved_to[axis : axis + 1, cols] = jnp.where(mine, disp + mean, 0.0)
            moved_to[3 + axis : 4 + axis, cols] = jnp.where(mine, pull, 0.0)
    for tile in range(16):
        cols = slice(tile * LANES, (tile + 1) * LANES)
        for r in range(3):
            even, odd = moved_to[2 * r : 2 * r + 1, cols], moved_to[2 * r + 1 : 2 * r + 2, cols]
            back[2 * tile, r : r + 1] = jnp.where(left, even, pltpu.roll(odd, 64, 1))
            back[2 * tile + 1, r : r + 1] = jnp.where(left, pltpu.roll(even, 64, 1), odd)


def third_kernel(force, zcat, xy, fluid, inside, outside, post, up, down, weighted, spread):
    for tile in range(8):
        cols = slice(tile * 256, (tile + 1) * 256)
        forces = [force[axis : axis + 1, cols] for axis in range(3)]
        weigh(weighted, xy[:, cols], forces, cols, CX * INNER)
    spread[...] = contract(weighted[...], zcat[...])
    for p, x in enumerate(INSIDE + OUTSIDE):
        base = inside if p < 2 else outside
        for tile in range(3):
            rows = slice(tile * 8, tile * 8 + 8)

            def put(i, value):
                post[i, x, rows] = value

            push = spread_at(spread, p * INNER + tile * 8, 8, CX * INNER, fluid[x, rows])
            forced(lambda i: base[i, p % 2, rows], push, put)
    for j, index in enumerate(UP):
        up[j] = moved(post[index, CX - 1], index, HALO - TRIM)[0:ROWS]
    for j, index in enumerate(DOWN):
        down[j] = moved(post[index, 0], index, HALO - TRIM)[0:ROWS]


def stream_kernel(post, out):
    for index in range(19):
        for x in range(CX):
            source = x - DIRS[index][0]
            if 0 <= source < CX:
                out[index, x] = moved(post[index, source], index, HALO - TRIM)[0:ROWS]
            else:
                out[index, x] = jnp.zeros((ROWS, NZ), F32)


def fill_kernel(part, up, down, out, sems):
    copies = []
    for j, index in enumerate(UP):
        copies.append(pltpu.make_async_copy(up.at[j], out.at[index, 0], sems.at[j]))
    for j, index in enumerate(DOWN):
        copies.append(pltpu.make_async_copy(down.at[j], out.at[index, CX - 1], sems.at[5 + j]))
    for copy in copies:
        copy.start()
    for copy in copies:
        copy.wait()


IN_VMEM = pl.BlockSpec(memory_space=pltpu.VMEM)
ANYWHERE = pl.BlockSpec(memory_space=pl.ANY)


def near(x):
    return pltpu.with_memory_space_constraint(x, pltpu.VMEM)


def run(kernel, args, outs, scratch=(), cost=4_000_000):
    return pl.pallas_call(
        kernel,
        out_shape=outs,
        in_specs=[IN_VMEM] * len(args),
        out_specs=jax.tree.map(lambda _: IN_VMEM, outs, is_leaf=lambda leaf: not isinstance(leaf, tuple)),
        scratch_shapes=list(scratch),
        compiler_params=pltpu.CompilerParams(vmem_limit_bytes=24 * 2**20),
        cost_estimate=pl.CostEstimate(flops=0, transcendentals=0, bytes_accessed=cost),
    )(*args)


def ring(axis):
    peers = lax.axis_size(axis)
    forward = [(i, (i + 1) % peers) for i in range(peers)]
    return forward, [(j, i) for i, j in forward]


def parts(populations, solid, marker_corner, marker_frac, marker_target, stiffness, displacement):
    peers = lax.axis_size("sub")
    sub_up, sub_down = ring("sub")
    plate_up, plate_down = ring("plate")
    args = (populations, solid, marker_corner, marker_frac, marker_target, stiffness.reshape(1, 64), displacement)
    shape = (20, CX, HALO, NZ)
    sent, bottom, top = pl.pallas_call(
        pack_kernel,
        out_shape=(
            jax.ShapeDtypeStruct((peers, 6, LANES), F32),
            pltpu.VMEM(shape, F32),
            pltpu.VMEM(shape, F32),
        ),
        in_specs=[pl.BlockSpec(memory_space=pltpu.HBM)] * 7,
        out_specs=[IN_VMEM] * 3,
        scratch_shapes=[
            pltpu.VMEM((8, LANES), F32),
            pltpu.VMEM(solid.shape, jnp.int32),
            *[pltpu.VMEM(arg.shape, arg.dtype) for arg in args[2:]],
            pltpu.SemaphoreType.DMA((8,)),
        ],
        compiler_params=pltpu.CompilerParams(vmem_limit_bytes=8 * 2**20),
        name="pack_kernel",
    )(*[pltpu.with_memory_space_constraint(arg, pltpu.HBM) for arg in args])
    markers = lax.all_to_all(sent, "sub", 0, 0, tiled=True)
    low = lax.ppermute(bottom, "sub", sub_up)
    high = lax.ppermute(top, "sub", sub_down)
    vcat, base, fluid, fluid_inner = run(
        relax_kernel,
        (near(low), near(top), near(bottom), near(high)),
        (
            pltpu.VMEM((3 * XY, 2 * NZ), BF16),
            pltpu.VMEM((19, CX, EXT, NZ), F32),
            pltpu.VMEM((CX, EXT, NZ), F32),
            pltpu.VMEM((CX, INNER, NZ), F32),
        ),
    )
    post, up, down, zcat, state = run(
        first_kernel,
        (near(markers), near(vcat), near(base), near(fluid)),
        (
            pltpu.VMEM((19, CX, EXT, NZ), F32),
            pltpu.VMEM((5, INNER, NZ), F32),
            pltpu.VMEM((5, INNER, NZ), F32),
            pltpu.VMEM((2 * NZ, MARKERS), BF16),
            pltpu.VMEM((16, MARKERS), F32),
        ),
        (
            pltpu.VMEM((XY, MARKERS), F32),
            pltpu.VMEM((6 * XY, MARKERS), BF16),
            pltpu.VMEM((6 * XY, 2 * NZ), F32),
        ),
    )
    up = lax.ppermute(up, "plate", plate_up)
    down = lax.ppermute(down, "plate", plate_down)
    edge, inside, found, xy = run(
        inner_kernel,
        (near(post), near(fluid_inner), near(state), near(zcat)),
        (
            pltpu.VMEM((19, 2, INNER, NZ), F32),
            pltpu.VMEM((19, 2, INNER, NZ), F32),
            pltpu.VMEM((8, MARKERS), F32),
            pltpu.VMEM((CX * INNER, MARKERS), F32),
        ),
        (pltpu.VMEM((19, 2, INNER, NZ), F32), pltpu.VMEM((6 * INNER, NZ), F32)),
        cost=12_000_000,
    )
    outside, force, back = run(
        second_kernel,
        (near(edge), near(up), near(down), near(fluid_inner), near(state), near(zcat), near(xy), near(found)),
        (
            pltpu.VMEM((19, 2, INNER, NZ), F32),
            pltpu.VMEM((8, MARKERS), F32),
            jax.ShapeDtypeStruct((peers, 3, LANES), F32),
        ),
        (pltpu.VMEM((6 * INNER, NZ), F32), pltpu.VMEM((8, MARKERS), F32)),
    )
    back = lax.all_to_all(back, "sub", 0, 0, tiled=True)
    post, up, down = run(
        third_kernel,
        (near(force), near(zcat), near(xy), near(fluid_inner), near(inside), near(outside)),
        (
            pltpu.VMEM((19, CX, INNER, NZ), F32),
            pltpu.VMEM((5, ROWS, NZ), F32),
            pltpu.VMEM((5, ROWS, NZ), F32),
        ),
        (pltpu.VMEM((6 * CX * INNER, MARKERS), BF16), pltpu.VMEM((6 * CX * INNER, 2 * NZ), F32)),
    )
    up = lax.ppermute(up, "plate", plate_up)
    down = lax.ppermute(down, "plate", plate_down)
    part = run(stream_kernel, (near(post),), jax.ShapeDtypeStruct((19, CX, ROWS, NZ), F32))
    out = pl.pallas_call(
        fill_kernel,
        out_shape=jax.ShapeDtypeStruct((19, CX, ROWS, NZ), F32),
        in_specs=[ANYWHERE, IN_VMEM, IN_VMEM],
        out_specs=ANYWHERE,
        scratch_shapes=[pltpu.SemaphoreType.DMA((10,))],
        input_output_aliases={0: 0},
        compiler_params=pltpu.CompilerParams(vmem_limit_bytes=8 * 2**20),
        name="fill_kernel",
    )(part, near(up), near(down))
    result = jnp.sum(back, 0).reshape(6, 64)
    return (out, result[:3], result[3:])


def solution(mesh):
    in_specs = (
        P(None, "plate", "sub", None),
        P("plate", "sub", None),
        P(None, ("plate", "sub")),
        P(None, ("plate", "sub")),
        P(None, ("plate", "sub")),
        P(("plate", "sub")),
        P(None, ("plate", "sub")),
    )
    out_specs = (
        P(None, "plate", "sub", None),
        P(None, ("plate", "sub")),
        P(None, ("plate", "sub")),
    )
    return jax.shard_map(parts, mesh=mesh, in_specs=in_specs, out_specs=out_specs, check_vma=False)
```

```python
import functools
import jax
import jax.numpy as jnp
from jax import lax
from jax.experimental import pallas as pl
from jax.experimental.pallas import tpu as pltpu
from jax.sharding import PartitionSpec as P

DIRS = [
    (0, 0, 0),
    (1, 0, 0),
    (-1, 0, 0),
    (0, 1, 0),
    (0, -1, 0),
    (0, 0, 1),
    (0, 0, -1),
    (1, 1, 0),
    (-1, -1, 0),
    (1, -1, 0),
    (-1, 1, 0),
    (1, 0, 1),
    (-1, 0, -1),
    (1, 0, -1),
    (-1, 0, 1),
    (0, 1, 1),
    (0, -1, -1),
    (0, 1, -1),
    (0, -1, 1),
]
WEIGHTS = [1.0 / 3.0] + [1.0 / 18.0] * 6 + [1.0 / 36.0] * 12
KAPPA = 4.0
RELAX = 0.9
UP = [i for i in range(19) if DIRS[i][0] == 1]
DOWN = [i for i in range(19) if DIRS[i][0] == -1]

CX = 4
ROWS = 16
HALO = 8
EXT = ROWS + 2 * HALO
NZ = 128
XY = CX * EXT
TRIM = 4
INNER = EXT - 2 * TRIM
MARKERS = 2048
VEL, FULL = 3, 5
AT_VEL, AT_PLANE = 8, 48
SENT_ROWS = AT_PLANE + 20 * CX * FULL + 8
KX, FORCE, STATE = 8, 12, 15
KY, KZ, WORK = 4, 8, 12
INSIDE, OUTSIDE = (1, 2), (0, 3)
LANES = 128
F32 = jnp.float32
BF16 = jnp.bfloat16


def split(value):
    high = value.astype(BF16)
    low = (value - high.astype(F32)).astype(BF16)
    return high, low


def moments_of(values):
    density = functools.reduce(lambda a, b: a + b, values)
    inverse = 1.0 / density
    velocity = []
    for axis in range(3):
        plus = functools.reduce(lambda a, b: a + b, [values[i] for i in range(19) if DIRS[i][axis] == 1])
        minus = functools.reduce(lambda a, b: a + b, [values[i] for i in range(19) if DIRS[i][axis] == -1])
        velocity.append((plus - minus) * inverse)
    return density, velocity


def along(index, vectors):
    total = None
    for axis in range(3):
        sign = DIRS[index][axis]
        if sign == 0:
            continue
        if total is None:
            total = vectors[axis] if sign == 1 else -vectors[axis]
        else:
            total = total + vectors[axis] if sign == 1 else total - vectors[axis]
    return total


def relaxed(values, density, velocity, fluid, put, indices=range(19)):
    keep, rate = 1.0 - 1.0 / RELAX, 1.0 / RELAX
    scaled = density * rate
    base = scaled - 1.5 * scaled * (
        velocity[0] * velocity[0] + velocity[1] * velocity[1] + velocity[2] * velocity[2]
    )
    if 0 in indices:
        put(0, jnp.where(fluid, keep * values[0] + WEIGHTS[0] * base, values[0]))
    for index in range(1, 19, 2):
        if index not in indices:
            continue
        weight = WEIGHTS[index]
        first, second = values[index], values[index + 1]
        proj = along(index, velocity)
        scaled_proj = scaled * proj
        even = weight * (base + 4.5 * scaled_proj * proj)
        odd = (3.0 * weight) * scaled_proj
        put(index, jnp.where(fluid, keep * first + (even + odd), second))
        put(index + 1, jnp.where(fluid, keep * second + (even - odd), first))


def forced(base, force, put, indices=range(19)):
    if 0 in indices:
        put(0, base(0))
    for index in range(1, 19, 2):
        if index not in indices:
            continue
        push = (3.0 * WEIGHTS[index]) * along(index, force)
        put(index, base(index) + push)
        put(index + 1, base(index + 1) - push)


def interpolated(velocity, zcat, cols):
    z_high, z_low = zcat[0:NZ, cols], zcat[NZ : 2 * NZ, cols]
    return jnp.dot(velocity, jnp.concatenate([z_high, z_high, z_low], 0), preferred_element_type=F32)


def tripled(velocity):
    high, low = split(velocity)
    return jnp.concatenate([high, low, high], 1)


def averaged(found, y_rows, kx):
    rows = y_rows.shape[0]
    total = None
    for p, weight in enumerate(kx):
        product = found[p * rows : (p + 1) * rows] * y_rows
        part = sum(product[t * 8 + 8 : t * 8 + 16] for t in range(rows // 8 - 1)) + product[0:8]
        total = part * weight if total is None else total + part * weight
    return jnp.sum(total, axis=0, keepdims=True)


def weigh(weighted, ys, forces, state, planes, rows):
    for tile in range(16):
        cols = slice(tile * LANES, (tile + 1) * LANES)
        y_rows = ys[:, cols]
        for axis in range(3):
            for p, x in enumerate(planes):
                scale = forces(axis, tile) * state[KX + x, tile : tile + 1]
                at = (axis * 2 + p) * rows
                high, low = split(y_rows * scale)
                weighted[at : at + rows, cols] = high
                weighted[6 * rows + at : 6 * rows + at + rows, cols] = low


def contract(weighted, zcat):
    return lax.dot_general(weighted, zcat, (((1,), (1,)), ((), ())), preferred_element_type=F32)


def spread_at(spread, p, tile, rows, fluid):
    result = []
    for axis in range(3):
        at = (axis * 2 + p) * rows + tile * 8
        low = 6 * rows + at
        whole = spread[at : at + 8, 0:NZ] + spread[at : at + 8, NZ : 2 * NZ]
        result.append((whole + spread[low : low + 8, 0:NZ]) * fluid)
    return result


def moved(block, index, offset):
    _, shift_y, shift_z = DIRS[index]
    shift_y = (shift_y - offset) % block.shape[0]
    if shift_y:
        block = pltpu.roll(block, shift_y, 0)
    if shift_z:
        block = pltpu.roll(block, shift_z % NZ, 1)
    return block


def pack_kernel(own, solid, corner, frac, target, stiffness, disp, sent, cells, bottom, top, block, walls, *held):
    sems = held[-1]
    held = held[:-1]
    small = [
        pltpu.make_async_copy(source, target_ref, sems.at[k])
        for k, (source, target_ref) in enumerate(zip((corner, frac, target, stiffness, disp), held))
    ]
    large = [
        pltpu.make_async_copy(solid, walls, sems.at[5]),
        pltpu.make_async_copy(own, cells.at[0:19], sems.at[6]),
    ]
    for copy in small + large:
        copy.start()
    for copy in small:
        copy.wait()
    corner, frac, target, stiffness, disp = held
    values = [corner[1:2].astype(F32), corner[2:3].astype(F32), frac[0:1], frac[1:2], frac[2:3], stiffness[...]]
    values += [target[axis : axis + 1] for axis in range(3)] + [disp[axis : axis + 1] for axis in range(3)]
    for r, value in enumerate(values):
        block[r // 2 : r // 2 + 1, 64 * (r % 2) : 64 * (r % 2) + 64] = value
    whole = block[0:6]
    peers = sent.shape[0]
    period = float(peers * ROWS)
    first = (lax.broadcasted_iota(jnp.int32, (6, LANES), 0) == 0) & (
        lax.broadcasted_iota(jnp.int32, (6, LANES), 1) < 64
    )
    for peer in range(peers):
        away = whole - float(peer * ROWS)
        away = away - jnp.where(away >= period / 2, period, jnp.where(away < -period / 2, -period, 0.0))
        sent[peer] = jnp.where(first, away, whole)
    for copy in large:
        copy.wait()
    for buffer in (bottom, top):
        for at in (0, AT_PLANE - 8, SENT_ROWS - 8):
            buffer[at : at + 8] = jnp.zeros((8, NZ), F32)
    for x in range(CX):
        cells[19, x] = walls[x].astype(F32)
        for buffer, rows, full, vel in ((bottom, slice(8, 16), 3, 0), (top, slice(0, 8), 0, 5)):
            values = [cells[i, x, rows] for i in range(20)]
            for i, value in enumerate(values):
                at = AT_PLANE + (i * CX + x) * FULL
                buffer[at : at + FULL] = value[full : full + FULL]
            for axis, value in enumerate(moments_of(values[0:19])[1]):
                at = AT_VEL + (axis * CX + x) * VEL
                buffer[at : at + VEL] = value[vel : vel + VEL]


def relax_kernel(low, cells, high, vcat, base, fluid, fluid_inner):
    row = lax.broadcasted_iota(jnp.int32, (8, NZ), 0)
    for x in range(CX):

        def before(i):
            at = AT_PLANE + (i * CX + x) * FULL - VEL
            return low[at : at + 8]

        def after(i):
            at = AT_PLANE + (i * CX + x) * FULL
            return high[at : at + 8]

        wall = jnp.concatenate([before(19), cells[19, x], after(19)], 0)
        is_fluid = 1.0 - wall
        fluid[x] = is_fluid
        fluid_inner[x] = pltpu.roll(is_fluid, EXT - TRIM, 0)[0:INNER]
        for half in range(2):
            rows = slice(half * 16, half * 16 + 16)

            def pop(i):
                if half == 0:
                    return jnp.concatenate([before(i), cells[i, x, 0:8]], 0)
                return jnp.concatenate([cells[i, x, 8:16], after(i)], 0)

            values = [pop(i) for i in range(19)]
            density, velocity = moments_of(values)
            for axis in range(3):
                at = AT_VEL + (axis * CX + x) * VEL
                if half == 0:
                    outer = jnp.where(row < VEL, low[at : at + 8], velocity[axis][0:8])
                    known = jnp.concatenate([outer, velocity[axis][8:16]], 0)
                else:
                    outer = jnp.where(row >= FULL, high[at - FULL : at - FULL + 8], velocity[axis][8:16])
                    known = jnp.concatenate([velocity[axis][0:8], outer], 0)
                at = axis * XY + x * EXT + half * 16
                vcat[at : at + 16, 0:NZ], vcat[at : at + 16, NZ:] = split(known)

            def put(i, value):
                base[i, x, rows] = value

            relaxed(values, density, velocity, is_fluid[rows] > 0.5, put)


def dense(cells, first, weights):
    offset = cells - first
    value = jnp.where(offset == 3.0, weights[3], 0.0)
    for k in (2, 1, 0):
        value = jnp.where(offset == float(k), weights[k], value)
    return value


def kernel_weights(frac):
    root = jnp.sqrt(1.0 + 4.0 * frac - 4.0 * frac * frac)
    second = (3.0 - 2.0 * frac + root) / 8.0
    third = (1.0 + 2.0 * frac + root) / 8.0
    return [0.5 - third, second, third, 0.5 - second]


def weights_kernel(markers, zcat, ys, state, work):
    left = lax.broadcasted_iota(jnp.int32, (6, LANES), 1) < 64
    for tile in range(16):
        one, two = markers[2 * tile], markers[2 * tile + 1]
        even = jnp.where(left, one, pltpu.roll(two, 64, 1))
        odd = jnp.where(left, pltpu.roll(one, 64, 1), two)
        kept = (even[3:4], odd[3:4], even[4:5], odd[2:3], odd[4:5], even[5:6], odd[5:6], even[0:1])
        for r, value in enumerate(kept):
            state[r, tile : tile + 1] = value
        for r, value in enumerate((odd[0:1], even[1:2], odd[1:2], even[2:3])):
            work[r, tile : tile + 1] = value
    for r, target, at in ((1, state, KX), (2, work, KY), (3, work, KZ)):
        for k, value in enumerate(kernel_weights(work[r])):
            target[at + k] = value

    z_cell = lax.broadcasted_iota(jnp.int32, (NZ, LANES), 0).astype(F32)
    y_cell = lax.broadcasted_iota(jnp.int32, (EXT, LANES), 0).astype(F32) - HALO
    for tile in range(16):
        cols = slice(tile * LANES, (tile + 1) * LANES)

        def row(r):
            return work[r, tile : tile + 1]

        zcat[0:NZ, cols], zcat[NZ : 2 * NZ, cols] = split(dense(z_cell, row(0), [row(KZ + k) for k in range(4)]))
        ys[:, cols] = dense(y_cell, state[7, tile : tile + 1], [row(KY + k) for k in range(4)])


def first_kernel(vcat, base, fluid, zcat, ys, given, up, down, push, state, work, weighted, spread):
    state[0:FORCE] = given[...]
    velocity = jnp.concatenate([vcat[...], vcat[:, 0:NZ]], 1)
    for pair in range(8):
        found = interpolated(velocity, zcat, slice(pair * 256, (pair + 1) * 256))
        for half in range(2):
            tile = 2 * pair + half
            for axis in range(3):
                work[axis, tile : tile + 1] = averaged(
                    found[axis * XY : (axis + 1) * XY, half * LANES : (half + 1) * LANES],
                    ys[:, tile * LANES : (tile + 1) * LANES],
                    [state[KX + x, tile : tile + 1] for x in range(CX)],
                )
    for axis in range(3):
        mean, disp = work[axis], state[4 + axis]
        state[FORCE + axis] = KAPPA * (state[axis] - mean) - state[3] * disp
        state[4 + axis] = disp + mean

    weigh(weighted, ys, lambda axis, tile: state[FORCE + axis, tile : tile + 1], state, OUTSIDE, EXT)
    spread[...] = contract(weighted[...], zcat[...])
    for p, x in enumerate(OUTSIDE):
        for tile in range(4):
            rows = slice(tile * 8, tile * 8 + 8)
            for axis, value in enumerate(spread_at(spread, p, tile, EXT, fluid[x, rows])):
                push[axis, p, rows] = value
    for p, faces, target in ((1, UP, up), (0, DOWN, down)):
        for j, index in enumerate(faces):
            force = along(index, [push[axis, p] for axis in range(3)])
            plane = base[index, OUTSIDE[p]] + (3.0 * WEIGHTS[index]) * force
            target[j] = moved(plane, index, TRIM)[0:INNER]


def inner_kernel(base, fluid, fluid_inner, push, ys, zcat, state, edge, found, inside, post, moving, velocities, weighted, spread):
    weigh(weighted, ys, lambda axis, tile: state[FORCE + axis, tile : tile + 1], state, INSIDE, EXT)
    spread[...] = contract(weighted[...], zcat[...])
    for x in range(CX):
        for tile in range(4):
            rows = slice(tile * 8, tile * 8 + 8)

            def put(i, value):
                post[i, x, rows] = value

            if x in INSIDE:
                force = spread_at(spread, x - 1, tile, EXT, fluid[x, rows])
            else:
                force = [push[axis, x // 3, rows] for axis in range(3)]
            forced(lambda i: base[i, x, rows], force, put)
    for index in range(19):
        for x in range(CX):
            source = x - DIRS[index][0]
            if not 0 <= source < CX:
                continue
            plane = moved(post[index, source], index, TRIM)[0:INNER]
            if x in INSIDE:
                moving[index, x - 1] = plane
            else:
                edge[index, x // 3] = plane
    for p, x in enumerate(INSIDE):
        for tile in range(3):
            rows = slice(tile * 8, tile * 8 + 8)
            values = [moving[i, p, rows] for i in range(19)]
            density, velocity = moments_of(values)
            for axis in range(3):
                at = (axis * 2 + p) * INNER + tile * 8
                velocities[at : at + 8] = velocity[axis]

            def put(i, value):
                inside[i, p, rows] = value

            relaxed(values, density, velocity, fluid_inner[x, rows] > 0.5, put)
    partial_means(velocities, zcat, ys, state, INSIDE, lambda axis, tile, value: found.__setitem__((axis, slice(tile, tile + 1)), value))


def partial_means(velocities, zcat, ys, state, planes, put):
    velocity = tripled(velocities[...])
    for pair in range(8):
        found = interpolated(velocity, zcat, slice(pair * 256, (pair + 1) * 256))
        for half in range(2):
            tile = 2 * pair + half
            y_rows = ys[TRIM : TRIM + INNER, tile * LANES : (tile + 1) * LANES]
            for axis in range(3):
                at = axis * 2 * INNER
                part = averaged(
                    found[at : at + 2 * INNER, half * LANES : (half + 1) * LANES],
                    y_rows,
                    [state[KX + x, tile : tile + 1] for x in planes],
                )
                put(axis, tile, part)


def edge_values(edge, up, down, x, rows):
    def value(i):
        if x == 0 and DIRS[i][0] == 1:
            return up[UP.index(i), rows]
        if x == CX - 1 and DIRS[i][0] == -1:
            return down[DOWN.index(i), rows]
        return edge[i, x // 3, rows]

    return [value(i) for i in range(19)]


def second_kernel(edge, up, down, ys, zcat, state, found, force, density, velocities, back, mean, rest):
    for p, x in enumerate(OUTSIDE):
        for tile in range(3):
            rows = slice(tile * 8, tile * 8 + 8)
            dense_at, velocity = moments_of(edge_values(edge, up, down, x, rows))
            density[p, rows] = dense_at
            for axis in range(3):
                at = (axis * 2 + p) * INNER + tile * 8
                velocities[at : at + 8] = velocity[axis]
    partial_means(velocities, zcat, ys, state, OUTSIDE, lambda axis, tile, value: mean.__setitem__((axis, slice(tile, tile + 1)), value))
    mine = (state[7] >= 0.0) & (state[7] < float(ROWS))
    moved_to, pulls = [], []
    for axis in range(3):
        average = found[axis] + mean[axis]
        disp = state[4 + axis]
        pull = KAPPA * (state[axis] - average) - state[3] * disp
        force[axis] = pull
        moved_to.append(jnp.where(mine, disp + average, 0.0))
        pulls.append(jnp.where(mine, pull, 0.0))
    values = moved_to + pulls
    left = lax.broadcasted_iota(jnp.int32, (16, LANES), 1) < 64
    for r in range(3):
        even, odd = values[2 * r], values[2 * r + 1]
        rest[0, r] = jnp.where(left, even, pltpu.roll(odd, 64, 1))
        rest[1, r] = jnp.where(left, pltpu.roll(even, 64, 1), odd)
        for tile in range(16):
            back[2 * tile, r : r + 1] = rest[0, r, tile : tile + 1]
            back[2 * tile + 1, r : r + 1] = rest[1, r, tile : tile + 1]


def third_kernel(
    edge, up, down, fluid, density, velocities, force, ys, zcat, state, out_up, out_down, post, weighted, spread, trimmed
):
    trimmed[...] = ys[TRIM : TRIM + INNER]
    weigh(weighted, trimmed, lambda axis, tile: force[axis, tile : tile + 1], state, OUTSIDE, INNER)
    spread[...] = contract(weighted[...], zcat[...])
    for p, x in enumerate(OUTSIDE):
        for tile in range(3):
            rows = slice(tile * 8, tile * 8 + 8)

            def put(i, value):
                post[i, p, rows] = value

            values = edge_values(edge, up, down, x, rows)
            velocity = [velocities[pl.ds((axis * 2 + p) * INNER + tile * 8, 8)] for axis in range(3)]
            is_fluid = fluid[x, rows]
            relaxed(values, density[p, rows], velocity, is_fluid > 0.5, put)
            pushed = spread_at(spread, p, tile, INNER, is_fluid)
            forced(lambda i: post[i, p, rows], pushed, put)
    for j, index in enumerate(UP):
        out_up[j] = moved(post[index, 1], index, HALO - TRIM)[0:ROWS]
    for j, index in enumerate(DOWN):
        out_down[j] = moved(post[index, 0], index, HALO - TRIM)[0:ROWS]


def stream_kernel(inside, outside, fluid, force, ys, zcat, state, out, post, weighted, spread, trimmed):
    trimmed[...] = ys[TRIM : TRIM + INNER]
    weigh(weighted, trimmed, lambda axis, tile: force[axis, tile : tile + 1], state, INSIDE, INNER)
    spread[...] = contract(weighted[...], zcat[...])
    for p, x in enumerate(INSIDE):
        for tile in range(3):
            rows = slice(tile * 8, tile * 8 + 8)

            def put(i, value):
                post[i, p, rows] = value

            forced(lambda i: inside[i, p, rows], spread_at(spread, p, tile, INNER, fluid[x, rows]), put)
    for index in range(19):
        for x in range(CX):
            source = x - DIRS[index][0]
            if 0 <= source < CX:
                plane = post[index, source - 1] if source in INSIDE else outside[index, source // 3]
                out[index, x] = moved(plane, index, HALO - TRIM)[0:ROWS]
            else:
                out[index, x] = jnp.zeros((ROWS, NZ), F32)


def fill_kernel(part, up, down, out, sems):
    copies = []
    for j, index in enumerate(UP):
        copies.append(pltpu.make_async_copy(up.at[j], out.at[index, 0], sems.at[j]))
    for j, index in enumerate(DOWN):
        copies.append(pltpu.make_async_copy(down.at[j], out.at[index, CX - 1], sems.at[5 + j]))
    for copy in copies:
        copy.start()
    for copy in copies:
        copy.wait()


IN_VMEM = pl.BlockSpec(memory_space=pltpu.VMEM)
ANYWHERE = pl.BlockSpec(memory_space=pl.ANY)


def near(x):
    return pltpu.with_memory_space_constraint(x, pltpu.VMEM)


def run(kernel, args, outs, scratch=(), cost=4_000_000):
    return pl.pallas_call(
        kernel,
        out_shape=outs,
        in_specs=[IN_VMEM] * len(args),
        out_specs=jax.tree.map(lambda _: IN_VMEM, outs, is_leaf=lambda leaf: not isinstance(leaf, tuple)),
        scratch_shapes=list(scratch),
        compiler_params=pltpu.CompilerParams(vmem_limit_bytes=24 * 2**20),
        cost_estimate=pl.CostEstimate(flops=0, transcendentals=0, bytes_accessed=cost),
    )(*args)


def ring(axis):
    peers = lax.axis_size(axis)
    forward = [(i, (i + 1) % peers) for i in range(peers)]
    return forward, [(j, i) for i, j in forward]


def parts(populations, solid, marker_corner, marker_frac, marker_target, stiffness, displacement):
    peers = lax.axis_size("sub")
    sub_up, sub_down = ring("sub")
    plate_up, plate_down = ring("plate")
    args = (populations, solid, marker_corner, marker_frac, marker_target, stiffness.reshape(1, 64), displacement)
    shape = (SENT_ROWS, NZ)
    sent, cells, bottom, top = pl.pallas_call(
        pack_kernel,
        out_shape=(
            jax.ShapeDtypeStruct((peers, 6, LANES), F32),
            pltpu.VMEM((20, CX, ROWS, NZ), F32),
            pltpu.VMEM(shape, F32),
            pltpu.VMEM(shape, F32),
        ),
        in_specs=[pl.BlockSpec(memory_space=pltpu.HBM)] * 7,
        out_specs=[IN_VMEM] * 4,
        scratch_shapes=[
            pltpu.VMEM((8, LANES), F32),
            pltpu.VMEM(solid.shape, jnp.int32),
            *[pltpu.VMEM(arg.shape, arg.dtype) for arg in args[2:]],
            pltpu.SemaphoreType.DMA((7,)),
        ],
        compiler_params=pltpu.CompilerParams(vmem_limit_bytes=8 * 2**20),
        name="pack_kernel",
    )(*[pltpu.with_memory_space_constraint(arg, pltpu.HBM) for arg in args])
    markers = lax.all_to_all(sent, "sub", 0, 0, tiled=True)
    low = lax.ppermute(bottom, "sub", sub_up)
    high = lax.ppermute(top, "sub", sub_down)
    zcat, ys, given = run(
        weights_kernel,
        (near(markers),),
        (
            pltpu.VMEM((2 * NZ, MARKERS), BF16),
            pltpu.VMEM((EXT, MARKERS), F32),
            pltpu.VMEM((FORCE, 16, LANES), F32),
        ),
        (pltpu.VMEM((WORK, 16, LANES), F32),),
    )
    vcat, base, fluid, fluid_inner = run(
        relax_kernel,
        (near(low), near(cells), near(high)),
        (
            pltpu.VMEM((3 * XY, 2 * NZ), BF16),
            pltpu.VMEM((19, CX, EXT, NZ), F32),
            pltpu.VMEM((CX, EXT, NZ), F32),
            pltpu.VMEM((CX, INNER, NZ), F32),
        ),
    )
    faces = (pltpu.VMEM((5, INNER, NZ), F32),) * 2
    plane_pairs = pltpu.VMEM((19, 2, INNER, NZ), F32)
    rows = pltpu.VMEM((3, 16, LANES), F32)

    def spreading(cells):
        return (pltpu.VMEM((12 * cells, MARKERS), BF16), pltpu.VMEM((12 * cells, 2 * NZ), F32))

    up, down, push, state = run(
        first_kernel,
        (near(vcat), near(base), near(fluid), near(zcat), near(ys), near(given)),
        (*faces, pltpu.VMEM((3, 2, EXT, NZ), F32), pltpu.VMEM((STATE, 16, LANES), F32)),
        (rows, *spreading(EXT)),
    )
    up = lax.ppermute(up, "plate", plate_up)
    down = lax.ppermute(down, "plate", plate_down)
    known = (near(ys), near(zcat), near(state))
    edge, found, inside = run(
        inner_kernel,
        (near(base), near(fluid), near(fluid_inner), near(push), *known),
        (plane_pairs, rows, pltpu.HBM((19, 2, INNER, NZ), F32)),
        (
            pltpu.VMEM((19, CX, EXT, NZ), F32),
            plane_pairs,
            pltpu.VMEM((6 * INNER, NZ), F32),
            *spreading(EXT),
        ),
        cost=12_000_000,
    )
    edges = (near(edge), near(up), near(down))
    force, density, velocities, back = run(
        second_kernel,
        (*edges, *known, near(found)),
        (
            rows,
            pltpu.VMEM((2, INNER, NZ), F32),
            pltpu.VMEM((6 * INNER, NZ), F32),
            jax.ShapeDtypeStruct((peers, 3, LANES), F32),
        ),
        (rows, pltpu.VMEM((2, 3, 16, LANES), F32)),
    )
    back = lax.all_to_all(back, "sub", 0, 0, tiled=True)
    trimmed = pltpu.VMEM((INNER, MARKERS), F32)
    up, down, outside = run(
        third_kernel,
        (*edges, near(fluid_inner), near(density), near(velocities), near(force), *known),
        (*[pltpu.VMEM((5, ROWS, NZ), F32)] * 2, plane_pairs),
        (*spreading(INNER), trimmed),
    )
    up = lax.ppermute(up, "plate", plate_up)
    down = lax.ppermute(down, "plate", plate_down)
    part = run(
        stream_kernel,
        (pltpu.with_memory_space_constraint(inside, pltpu.HBM), near(outside), near(fluid_inner), near(force), *known),
        jax.ShapeDtypeStruct((19, CX, ROWS, NZ), F32),
        (plane_pairs, *spreading(INNER), trimmed),
        cost=12_000_000,
    )
    out = pl.pallas_call(
        fill_kernel,
        out_shape=jax.ShapeDtypeStruct((19, CX, ROWS, NZ), F32),
        in_specs=[ANYWHERE, IN_VMEM, IN_VMEM],
        out_specs=ANYWHERE,
        scratch_shapes=[pltpu.SemaphoreType.DMA((10,))],
        input_output_aliases={0: 0},
        compiler_params=pltpu.CompilerParams(vmem_limit_bytes=8 * 2**20),
        name="fill_kernel",
    )(part, near(up), near(down))
    result = jnp.sum(back, 0).reshape(6, 64)
    return (out, result[:3], result[3:])


def solution(mesh):
    in_specs = (
        P(None, "plate", "sub", None),
        P("plate", "sub", None),
        P(None, ("plate", "sub")),
        P(None, ("plate", "sub")),
        P(None, ("plate", "sub")),
        P(("plate", "sub")),
        P(None, ("plate", "sub")),
    )
    out_specs = (
        P(None, "plate", "sub", None),
        P(None, ("plate", "sub")),
        P(None, ("plate", "sub")),
    )
    return jax.shard_map(parts, mesh=mesh, in_specs=in_specs, out_specs=out_specs, check_vma=False)
```

```python
import functools
import jax
import jax.numpy as jnp
from jax import lax
from jax.experimental import pallas as pl
from jax.experimental.pallas import tpu as pltpu
from jax.sharding import PartitionSpec as P

DIRS = [
    (0, 0, 0),
    (1, 0, 0),
    (-1, 0, 0),
    (0, 1, 0),
    (0, -1, 0),
    (0, 0, 1),
    (0, 0, -1),
    (1, 1, 0),
    (-1, -1, 0),
    (1, -1, 0),
    (-1, 1, 0),
    (1, 0, 1),
    (-1, 0, -1),
    (1, 0, -1),
    (-1, 0, 1),
    (0, 1, 1),
    (0, -1, -1),
    (0, 1, -1),
    (0, -1, 1),
]
WEIGHTS = [1.0 / 3.0] + [1.0 / 18.0] * 6 + [1.0 / 36.0] * 12
KAPPA = 4.0
RELAX = 0.9
UP = [i for i in range(19) if DIRS[i][0] == 1]
DOWN = [i for i in range(19) if DIRS[i][0] == -1]

CX = 4
ROWS = 16
HALO = 8
EXT = ROWS + 2 * HALO
NZ = 128
TRIM = 4
INNER = EXT - 2 * TRIM
MARKERS = 2048
VEL, FULL = 3, 5
AT_VEL, AT_PLANE = 8, 48
SENT_ROWS = AT_PLANE + 20 * CX * FULL + 8
KX, FORCE, STATE = 8, 12, 15
KY, KZ, WORK = 4, 8, 12
INSIDE, OUTSIDE = (1, 2), (0, 3)
LANES = 128
F32 = jnp.float32
BF16 = jnp.bfloat16


def split(value):
    high = value.astype(BF16)
    low = (value - high.astype(F32)).astype(BF16)
    return high, low


def moments_of(values):
    density = functools.reduce(lambda a, b: a + b, values)
    inverse = 1.0 / density
    velocity = []
    for axis in range(3):
        plus = functools.reduce(lambda a, b: a + b, [values[i] for i in range(19) if DIRS[i][axis] == 1])
        minus = functools.reduce(lambda a, b: a + b, [values[i] for i in range(19) if DIRS[i][axis] == -1])
        velocity.append((plus - minus) * inverse)
    return density, velocity


def along(index, vectors):
    total = None
    for axis in range(3):
        sign = DIRS[index][axis]
        if sign == 0:
            continue
        if total is None:
            total = vectors[axis] if sign == 1 else -vectors[axis]
        else:
            total = total + vectors[axis] if sign == 1 else total - vectors[axis]
    return total


def relaxed(values, density, velocity, fluid, put, indices=range(19)):
    keep, rate = 1.0 - 1.0 / RELAX, 1.0 / RELAX
    scaled = density * rate
    base = scaled - 1.5 * scaled * (
        velocity[0] * velocity[0] + velocity[1] * velocity[1] + velocity[2] * velocity[2]
    )
    if 0 in indices:
        put(0, jnp.where(fluid, keep * values[0] + WEIGHTS[0] * base, values[0]))
    for index in range(1, 19, 2):
        if index not in indices:
            continue
        weight = WEIGHTS[index]
        first, second = values[index], values[index + 1]
        proj = along(index, velocity)
        scaled_proj = scaled * proj
        even = weight * (base + 4.5 * scaled_proj * proj)
        odd = (3.0 * weight) * scaled_proj
        put(index, jnp.where(fluid, keep * first + (even + odd), second))
        put(index + 1, jnp.where(fluid, keep * second + (even - odd), first))


def forced(base, force, put, indices=range(19)):
    if 0 in indices:
        put(0, base(0))
    for index in range(1, 19, 2):
        if index not in indices:
            continue
        push = (3.0 * WEIGHTS[index]) * along(index, force)
        put(index, base(index) + push)
        put(index + 1, base(index + 1) - push)


def interpolated(velocity, zcat, cols):
    z_high, z_low = zcat[0:NZ, cols], zcat[NZ : 2 * NZ, cols]
    return jnp.dot(velocity, jnp.concatenate([z_high, z_high, z_low], 0), preferred_element_type=F32)


def tripled(velocity):
    high, low = split(velocity)
    return jnp.concatenate([high, low, high], 1)


def averaged(found, y_rows, kx):
    rows = y_rows.shape[0]
    total = None
    for p, weight in enumerate(kx):
        product = found[p * rows : (p + 1) * rows] * y_rows
        part = sum(product[t * 8 + 8 : t * 8 + 16] for t in range(rows // 8 - 1)) + product[0:8]
        total = part * weight if total is None else total + part * weight
    return jnp.sum(total, axis=0, keepdims=True)


def weigh(weighted, ys, forces, state, planes, rows):
    for tile in range(16):
        cols = slice(tile * LANES, (tile + 1) * LANES)
        y_rows = ys[:, cols]
        for axis in range(3):
            for p, x in enumerate(planes):
                scale = forces(axis, tile) * state[KX + x, tile : tile + 1]
                at = (axis * 2 + p) * rows
                high, low = split(y_rows * scale)
                weighted[at : at + rows, cols] = high
                weighted[6 * rows + at : 6 * rows + at + rows, cols] = low


def contract(weighted, zcat):
    return lax.dot_general(weighted, zcat, (((1,), (1,)), ((), ())), preferred_element_type=F32)


def spread_at(spread, p, tile, rows, fluid):
    result = []
    for axis in range(3):
        at = (axis * 2 + p) * rows + tile * 8
        low = 6 * rows + at
        whole = spread[at : at + 8, 0:NZ] + spread[at : at + 8, NZ : 2 * NZ]
        result.append((whole + spread[low : low + 8, 0:NZ]) * fluid)
    return result


def moved(block, index, offset):
    _, shift_y, shift_z = DIRS[index]
    shift_y = (shift_y - offset) % block.shape[0]
    if shift_y:
        block = pltpu.roll(block, shift_y, 0)
    if shift_z:
        block = pltpu.roll(block, shift_z % NZ, 1)
    return block


def pack_kernel(own, solid, corner, frac, target, stiffness, disp, sent, cells, bottom, top, block, walls, blocks, *held):
    sems = held[-1]
    held = held[:-1]
    small = [
        pltpu.make_async_copy(source, target_ref, sems.at[k])
        for k, (source, target_ref) in enumerate(zip((corner, frac, target, stiffness, disp), held))
    ]
    large = [
        pltpu.make_async_copy(solid, walls, sems.at[5]),
        pltpu.make_async_copy(own, cells.at[0:19], sems.at[6]),
    ]
    for copy in small + large:
        copy.start()
    for copy in small:
        copy.wait()
    corner, frac, target, stiffness, disp = held
    values = [corner[1:2].astype(F32), corner[2:3].astype(F32), frac[0:1], frac[1:2], frac[2:3], stiffness[...]]
    values += [target[axis : axis + 1] for axis in range(3)] + [disp[axis : axis + 1] for axis in range(3)]
    for r, value in enumerate(values):
        block[r // 2 : r // 2 + 1, 64 * (r % 2) : 64 * (r % 2) + 64] = value
    whole = block[0:6]
    peers = sent.shape[0]
    period = float(peers * ROWS)
    first = (lax.broadcasted_iota(jnp.int32, (6, LANES), 0) == 0) & (
        lax.broadcasted_iota(jnp.int32, (6, LANES), 1) < 64
    )
    for peer in range(peers):
        away = whole - float(peer * ROWS)
        away = away - jnp.where(away >= period / 2, period, jnp.where(away < -period / 2, -period, 0.0))
        blocks[peer] = jnp.where(first, away, whole)
    going = pltpu.make_async_copy(blocks, sent, sems.at[7])
    going.start()
    for copy in large:
        copy.wait()
    for buffer in (bottom, top):
        for at in (0, AT_PLANE - 8, SENT_ROWS - 8):
            buffer[at : at + 8] = jnp.zeros((8, NZ), F32)
    for x in range(CX):
        cells[19, x] = walls[x].astype(F32)
        for buffer, rows, full, vel in ((bottom, slice(8, 16), 3, 0), (top, slice(0, 8), 0, 5)):
            values = [cells[i, x, rows] for i in range(20)]
            for i, value in enumerate(values):
                at = AT_PLANE + (i * CX + x) * FULL
                buffer[at : at + FULL] = value[full : full + FULL]
            for axis, value in enumerate(moments_of(values[0:19])[1]):
                at = AT_VEL + (axis * CX + x) * VEL
                buffer[at : at + VEL] = value[vel : vel + VEL]
    going.wait()


def own_kernel(cells, vcat, base, walls):
    for x in range(CX):
        walls[x] = cells[19, x]
        values = [cells[i, x] for i in range(19)]
        density, velocity = moments_of(values)
        for axis in range(3):
            at = (axis * CX + x) * ROWS
            vcat[at : at + ROWS, 0:NZ], vcat[at : at + ROWS, NZ:] = split(velocity[axis])

        def put(i, value):
            base[i, x] = value

        relaxed(values, density, velocity, cells[19, x] < 0.5, put)


def outer_kernel(low, walls, high, vcat, base, fluid, fluid_inner):
    row = lax.broadcasted_iota(jnp.int32, (16, NZ), 0)
    received = (row < VEL) | (row >= HALO + FULL)
    for x in range(CX):

        def pop(i):
            at = AT_PLANE + (i * CX + x) * FULL
            return jnp.concatenate([low[at - VEL : at - VEL + 8], high[at : at + 8]], 0)

        wall = pop(19)
        is_fluid = 1.0 - jnp.concatenate([wall[0:8], walls[x], wall[8:16]], 0)
        fluid[x] = is_fluid
        fluid_inner[x] = pltpu.roll(is_fluid, EXT - TRIM, 0)[0:INNER]
        values = [pop(i) for i in range(19)]
        density, velocity = moments_of(values)
        for axis in range(3):
            at = AT_VEL + (axis * CX + x) * VEL
            sent = jnp.concatenate([low[at : at + 8], high[at - FULL : at - FULL + 8]], 0)
            known = jnp.where(received, sent, velocity[axis])
            at = (axis * CX + x) * ROWS
            vcat[at : at + ROWS, 0:NZ], vcat[at : at + ROWS, NZ:] = split(known)

        def put(i, value):
            base[i, x] = value

        relaxed(values, density, velocity, wall < 0.5, put)


def dense(cells, first, weights):
    offset = cells - first
    value = jnp.where(offset == 3.0, weights[3], 0.0)
    for k in (2, 1, 0):
        value = jnp.where(offset == float(k), weights[k], value)
    return value


def kernel_weights(frac):
    root = jnp.sqrt(1.0 + 4.0 * frac - 4.0 * frac * frac)
    second = (3.0 - 2.0 * frac + root) / 8.0
    third = (1.0 + 2.0 * frac + root) / 8.0
    return [0.5 - third, second, third, 0.5 - second]


def weights_kernel(markers, zcat, ys, state, work):
    left = lax.broadcasted_iota(jnp.int32, (6, LANES), 1) < 64
    for tile in range(16):
        one, two = markers[2 * tile], markers[2 * tile + 1]
        even = jnp.where(left, one, pltpu.roll(two, 64, 1))
        odd = jnp.where(left, pltpu.roll(one, 64, 1), two)
        kept = (even[3:4], odd[3:4], even[4:5], odd[2:3], odd[4:5], even[5:6], odd[5:6], even[0:1])
        for r, value in enumerate(kept):
            state[r, tile : tile + 1] = value
        for r, value in enumerate((odd[0:1], even[1:2], odd[1:2], even[2:3])):
            work[r, tile : tile + 1] = value
    for r, target, at in ((1, state, KX), (2, work, KY), (3, work, KZ)):
        for k, value in enumerate(kernel_weights(work[r])):
            target[at + k] = value

    z_cell = lax.broadcasted_iota(jnp.int32, (NZ, LANES), 0).astype(F32)
    y_cell = lax.broadcasted_iota(jnp.int32, (EXT, LANES), 0).astype(F32) - HALO
    for tile in range(16):
        cols = slice(tile * LANES, (tile + 1) * LANES)

        def row(r):
            return work[r, tile : tile + 1]

        zcat[0:NZ, cols], zcat[NZ : 2 * NZ, cols] = split(dense(z_cell, row(0), [row(KZ + k) for k in range(4)]))
        ys[:, cols] = dense(y_cell, state[7, tile : tile + 1], [row(KY + k) for k in range(4)])


def first_kernel(
    vown, vouter, own, outer, fluid, zcat, ys, given, up, down, push, state, work, weighted, spread
):
    state[0:FORCE] = given[...]
    velocity = jnp.concatenate([vown[...], vouter[...]], 0)
    velocity = jnp.concatenate([velocity, velocity[:, 0:NZ]], 1)
    for pair in range(8):
        found = interpolated(velocity, zcat, slice(pair * 256, (pair + 1) * 256))
        for half in range(2):
            tile = 2 * pair + half
            for axis in range(3):
                at, lanes = axis * CX * ROWS, slice(half * LANES, (half + 1) * LANES)
                cols = slice(tile * LANES, (tile + 1) * LANES)
                kx = [state[KX + x, tile : tile + 1] for x in range(CX)]
                inner = averaged(found[at : at + CX * ROWS, lanes], ys[HALO : HALO + ROWS, cols], kx)
                y_outer = jnp.concatenate([ys[0:HALO, cols], ys[HALO + ROWS :, cols]], 0)
                at += 3 * CX * ROWS
                work[axis, tile : tile + 1] = inner + averaged(found[at : at + CX * ROWS, lanes], y_outer, kx)
    for axis in range(3):
        mean, disp = work[axis], state[4 + axis]
        state[FORCE + axis] = KAPPA * (state[axis] - mean) - state[3] * disp
        state[4 + axis] = disp + mean

    weigh(weighted, ys, lambda axis, tile: state[FORCE + axis, tile : tile + 1], state, OUTSIDE, EXT)
    spread[...] = contract(weighted[...], zcat[...])
    for p, x in enumerate(OUTSIDE):
        for tile in range(4):
            rows = slice(tile * 8, tile * 8 + 8)
            for axis, value in enumerate(spread_at(spread, p, tile, EXT, fluid[x, rows])):
                push[axis, p, rows] = value
    for p, faces, target in ((1, UP, up), (0, DOWN, down)):
        for j, index in enumerate(faces):
            force = along(index, [push[axis, p] for axis in range(3)])
            x = OUTSIDE[p]
            plane = jnp.concatenate([outer[index, x, 0:HALO], own[index, x], outer[index, x, HALO:]], 0)
            plane = plane + (3.0 * WEIGHTS[index]) * force
            target[j] = moved(plane, index, TRIM)[0:INNER]


def inner_kernel(
    own, outer, fluid, fluid_inner, push, ys, zcat, state, edge, found, inside, trimmed, post, moving, velocities, weighted, spread
):
    trimmed[...] = ys[TRIM : TRIM + INNER]
    weigh(weighted, ys, lambda axis, tile: state[FORCE + axis, tile : tile + 1], state, INSIDE, EXT)
    spread[...] = contract(weighted[...], zcat[...])
    for x in range(CX):
        for tile in range(4):
            rows = slice(tile * 8, tile * 8 + 8)

            def put(i, value):
                post[i, x, rows] = value

            if x in INSIDE:
                force = spread_at(spread, x - 1, tile, EXT, fluid[x, rows])
            else:
                force = [push[axis, x // 3, rows] for axis in range(3)]

            def base(i):
                if tile in (0, 3):
                    return outer[i, x, 0:8] if tile == 0 else outer[i, x, 8:16]
                return own[i, x, tile * 8 - 8 : tile * 8]

            forced(base, force, put)
    for index in range(19):
        for x in range(CX):
            source = x - DIRS[index][0]
            if not 0 <= source < CX:
                continue
            plane = moved(post[index, source], index, TRIM)[0:INNER]
            if x in INSIDE:
                moving[index, x - 1] = plane
            else:
                edge[index, x // 3] = plane
    for p, x in enumerate(INSIDE):
        for tile in range(3):
            rows = slice(tile * 8, tile * 8 + 8)
            values = [moving[i, p, rows] for i in range(19)]
            density, velocity = moments_of(values)
            for axis in range(3):
                at = (axis * 2 + p) * INNER + tile * 8
                velocities[at : at + 8] = velocity[axis]

            def put(i, value):
                inside[i, p, rows] = value

            relaxed(values, density, velocity, fluid_inner[x, rows] > 0.5, put)
    partial_means(velocities, zcat, trimmed, state, INSIDE, lambda axis, tile, value: found.__setitem__((axis, slice(tile, tile + 1)), value))


def partial_means(velocities, zcat, ys, state, planes, put):
    velocity = tripled(velocities[...])
    for pair in range(8):
        found = interpolated(velocity, zcat, slice(pair * 256, (pair + 1) * 256))
        for half in range(2):
            tile = 2 * pair + half
            y_rows = ys[:, tile * LANES : (tile + 1) * LANES]
            for axis in range(3):
                at = axis * 2 * INNER
                part = averaged(
                    found[at : at + 2 * INNER, half * LANES : (half + 1) * LANES],
                    y_rows,
                    [state[KX + x, tile : tile + 1] for x in planes],
                )
                put(axis, tile, part)


def edge_values(edge, up, down, x, rows):
    def value(i):
        if x == 0 and DIRS[i][0] == 1:
            return up[UP.index(i), rows]
        if x == CX - 1 and DIRS[i][0] == -1:
            return down[DOWN.index(i), rows]
        return edge[i, x // 3, rows]

    return [value(i) for i in range(19)]


def second_kernel(edge, up, down, ys, zcat, state, found, force, density, velocities, back, mean, rest):
    for p, x in enumerate(OUTSIDE):
        for tile in range(3):
            rows = slice(tile * 8, tile * 8 + 8)
            dense_at, velocity = moments_of(edge_values(edge, up, down, x, rows))
            density[p, rows] = dense_at
            for axis in range(3):
                at = (axis * 2 + p) * INNER + tile * 8
                velocities[at : at + 8] = velocity[axis]
    partial_means(velocities, zcat, ys, state, OUTSIDE, lambda axis, tile, value: mean.__setitem__((axis, slice(tile, tile + 1)), value))
    mine = (state[7] >= 0.0) & (state[7] < float(ROWS))
    moved_to, pulls = [], []
    for axis in range(3):
        average = found[axis] + mean[axis]
        disp = state[4 + axis]
        pull = KAPPA * (state[axis] - average) - state[3] * disp
        force[axis] = pull
        moved_to.append(jnp.where(mine, disp + average, 0.0))
        pulls.append(jnp.where(mine, pull, 0.0))
    values = moved_to + pulls
    left = lax.broadcasted_iota(jnp.int32, (16, LANES), 1) < 64
    for r in range(3):
        even, odd = values[2 * r], values[2 * r + 1]
        rest[0, r] = jnp.where(left, even, pltpu.roll(odd, 64, 1))
        rest[1, r] = jnp.where(left, pltpu.roll(even, 64, 1), odd)
        for tile in range(16):
            back[2 * tile, r : r + 1] = rest[0, r, tile : tile + 1]
            back[2 * tile + 1, r : r + 1] = rest[1, r, tile : tile + 1]


def third_kernel(
    edge, up, down, fluid, density, velocities, force, ys, zcat, state, out_up, out_down, post, weighted, spread
):
    weigh(weighted, ys, lambda axis, tile: force[axis, tile : tile + 1], state, OUTSIDE, INNER)
    spread[...] = contract(weighted[...], zcat[...])
    for p, x in enumerate(OUTSIDE):
        for tile in range(3):
            rows = slice(tile * 8, tile * 8 + 8)

            def put(i, value):
                post[i, p, rows] = value

            values = edge_values(edge, up, down, x, rows)
            velocity = [velocities[pl.ds((axis * 2 + p) * INNER + tile * 8, 8)] for axis in range(3)]
            is_fluid = fluid[x, rows]
            relaxed(values, density[p, rows], velocity, is_fluid > 0.5, put)
            pushed = spread_at(spread, p, tile, INNER, is_fluid)
            forced(lambda i: post[i, p, rows], pushed, put)
    for j, index in enumerate(UP):
        out_up[j] = moved(post[index, 1], index, HALO - TRIM)[0:ROWS]
    for j, index in enumerate(DOWN):
        out_down[j] = moved(post[index, 0], index, HALO - TRIM)[0:ROWS]


def stream_kernel(inside, outside, fluid, force, ys, zcat, state, out, post, weighted, spread):
    weigh(weighted, ys, lambda axis, tile: force[axis, tile : tile + 1], state, INSIDE, INNER)
    spread[...] = contract(weighted[...], zcat[...])
    for p, x in enumerate(INSIDE):
        for tile in range(3):
            rows = slice(tile * 8, tile * 8 + 8)

            def put(i, value):
                post[i, p, rows] = value

            forced(lambda i: inside[i, p, rows], spread_at(spread, p, tile, INNER, fluid[x, rows]), put)
    for index in range(19):
        for x in range(CX):
            source = x - DIRS[index][0]
            if 0 <= source < CX:
                plane = post[index, source - 1] if source in INSIDE else outside[index, source // 3]
                out[index, x] = moved(plane, index, HALO - TRIM)[0:ROWS]
            else:
                out[index, x] = jnp.zeros((ROWS, NZ), F32)


def fill_kernel(part, up, down, out, sems):
    copies = []
    for j, index in enumerate(UP):
        copies.append(pltpu.make_async_copy(up.at[j], out.at[index, 0], sems.at[j]))
    for j, index in enumerate(DOWN):
        copies.append(pltpu.make_async_copy(down.at[j], out.at[index, CX - 1], sems.at[5 + j]))
    for copy in copies:
        copy.start()
    for copy in copies:
        copy.wait()


IN_VMEM = pl.BlockSpec(memory_space=pltpu.VMEM)
ANYWHERE = pl.BlockSpec(memory_space=pl.ANY)


def near(x):
    return pltpu.with_memory_space_constraint(x, pltpu.VMEM)


def run(kernel, args, outs, scratch=(), cost=4_000_000):
    return pl.pallas_call(
        kernel,
        out_shape=outs,
        in_specs=[IN_VMEM] * len(args),
        out_specs=jax.tree.map(lambda _: IN_VMEM, outs, is_leaf=lambda leaf: not isinstance(leaf, tuple)),
        scratch_shapes=list(scratch),
        compiler_params=pltpu.CompilerParams(vmem_limit_bytes=24 * 2**20),
        cost_estimate=pl.CostEstimate(flops=0, transcendentals=0, bytes_accessed=cost),
    )(*args)


def ring(axis):
    peers = lax.axis_size(axis)
    forward = [(i, (i + 1) % peers) for i in range(peers)]
    return forward, [(j, i) for i, j in forward]


def parts(populations, solid, marker_corner, marker_frac, marker_target, stiffness, displacement):
    peers = lax.axis_size("sub")
    sub_up, sub_down = ring("sub")
    plate_up, plate_down = ring("plate")
    args = (populations, solid, marker_corner, marker_frac, marker_target, stiffness.reshape(1, 64), displacement)
    shape = (SENT_ROWS, NZ)
    sent, cells, bottom, top = pl.pallas_call(
        pack_kernel,
        out_shape=(
            jax.ShapeDtypeStruct((peers, 6, LANES), F32),
            pltpu.VMEM((20, CX, ROWS, NZ), F32),
            pltpu.VMEM(shape, F32),
            pltpu.VMEM(shape, F32),
        ),
        in_specs=[pl.BlockSpec(memory_space=pltpu.HBM)] * 7,
        out_specs=[pl.BlockSpec(memory_space=pltpu.HBM), *[IN_VMEM] * 3],
        scratch_shapes=[
            pltpu.VMEM((8, LANES), F32),
            pltpu.VMEM(solid.shape, jnp.int32),
            pltpu.VMEM((peers, 6, LANES), F32),
            *[pltpu.VMEM(arg.shape, arg.dtype) for arg in args[2:]],
            pltpu.SemaphoreType.DMA((8,)),
        ],
        compiler_params=pltpu.CompilerParams(vmem_limit_bytes=8 * 2**20),
        name="pack_kernel",
    )(*[pltpu.with_memory_space_constraint(arg, pltpu.HBM) for arg in args])
    markers = lax.all_to_all(sent, "sub", 0, 0, tiled=True)
    low = lax.ppermute(bottom, "sub", sub_up)
    high = lax.ppermute(top, "sub", sub_down)
    zcat, ys, given = run(
        weights_kernel,
        (near(markers),),
        (
            pltpu.VMEM((2 * NZ, MARKERS), BF16),
            pltpu.VMEM((EXT, MARKERS), F32),
            pltpu.VMEM((FORCE, 16, LANES), F32),
        ),
        (pltpu.VMEM((WORK, 16, LANES), F32),),
    )
    half = (pltpu.VMEM((3 * CX * ROWS, 2 * NZ), BF16), pltpu.VMEM((19, CX, ROWS, NZ), F32))
    vown, own, walls = run(own_kernel, (near(cells),), (*half, pltpu.VMEM((CX, ROWS, NZ), F32)))
    vouter, outer, fluid, fluid_inner = run(
        outer_kernel,
        (near(low), near(walls), near(high)),
        (*half, pltpu.VMEM((CX, EXT, NZ), F32), pltpu.VMEM((CX, INNER, NZ), F32)),
    )
    faces = (pltpu.VMEM((5, INNER, NZ), F32),) * 2
    plane_pairs = pltpu.VMEM((19, 2, INNER, NZ), F32)
    rows = pltpu.VMEM((3, 16, LANES), F32)

    def spreading(cells):
        return (pltpu.VMEM((12 * cells, MARKERS), BF16), pltpu.VMEM((12 * cells, 2 * NZ), F32))

    up, down, push, state = run(
        first_kernel,
        (near(vown), near(vouter), near(own), near(outer), near(fluid), near(zcat), near(ys), near(given)),
        (*faces, pltpu.VMEM((3, 2, EXT, NZ), F32), pltpu.VMEM((STATE, 16, LANES), F32)),
        (rows, *spreading(EXT)),
    )
    up = lax.ppermute(up, "plate", plate_up)
    down = lax.ppermute(down, "plate", plate_down)
    known = (near(ys), near(zcat), near(state))
    trimmed = pltpu.VMEM((INNER, MARKERS), F32)
    edge, found, inside, ys = run(
        inner_kernel,
        (near(own), near(outer), near(fluid), near(fluid_inner), near(push), *known),
        (plane_pairs, rows, pltpu.HBM((19, 2, INNER, NZ), F32), trimmed),
        (
            pltpu.VMEM((19, CX, EXT, NZ), F32),
            plane_pairs,
            pltpu.VMEM((6 * INNER, NZ), F32),
            *spreading(EXT),
        ),
        cost=12_000_000,
    )
    known = (near(ys), near(zcat), near(state))
    edges = (near(edge), near(up), near(down))
    force, density, velocities, back = run(
        second_kernel,
        (*edges, *known, near(found)),
        (
            rows,
            pltpu.VMEM((2, INNER, NZ), F32),
            pltpu.VMEM((6 * INNER, NZ), F32),
            jax.ShapeDtypeStruct((peers, 3, LANES), F32),
        ),
        (rows, pltpu.VMEM((2, 3, 16, LANES), F32)),
    )
    back = lax.all_to_all(back, "sub", 0, 0, tiled=True)
    up, down, outside = run(
        third_kernel,
        (*edges, near(fluid_inner), near(density), near(velocities), near(force), *known),
        (*[pltpu.VMEM((5, ROWS, NZ), F32)] * 2, plane_pairs),
        spreading(INNER),
    )
    up = lax.ppermute(up, "plate", plate_up)
    down = lax.ppermute(down, "plate", plate_down)
    part = run(
        stream_kernel,
        (pltpu.with_memory_space_constraint(inside, pltpu.HBM), near(outside), near(fluid_inner), near(force), *known),
        jax.ShapeDtypeStruct((19, CX, ROWS, NZ), F32),
        (plane_pairs, *spreading(INNER)),
        cost=12_000_000,
    )
    out = pl.pallas_call(
        fill_kernel,
        out_shape=jax.ShapeDtypeStruct((19, CX, ROWS, NZ), F32),
        in_specs=[ANYWHERE, IN_VMEM, IN_VMEM],
        out_specs=ANYWHERE,
        scratch_shapes=[pltpu.SemaphoreType.DMA((10,))],
        input_output_aliases={0: 0},
        compiler_params=pltpu.CompilerParams(vmem_limit_bytes=8 * 2**20),
        name="fill_kernel",
    )(part, near(up), near(down))
    result = jnp.sum(back, 0).reshape(6, 64)
    return (out, result[:3], result[3:])


def solution(mesh):
    in_specs = (
        P(None, "plate", "sub", None),
        P("plate", "sub", None),
        P(None, ("plate", "sub")),
        P(None, ("plate", "sub")),
        P(None, ("plate", "sub")),
        P(("plate", "sub")),
        P(None, ("plate", "sub")),
    )
    out_specs = (
        P(None, "plate", "sub", None),
        P(None, ("plate", "sub")),
        P(None, ("plate", "sub")),
    )
    return jax.shard_map(parts, mesh=mesh, in_specs=in_specs, out_specs=out_specs, check_vma=False)
```

```python
import functools
import jax
import jax.numpy as jnp
from jax import lax
from jax.experimental import pallas as pl
from jax.experimental.pallas import tpu as pltpu
from jax.sharding import PartitionSpec as P

DIRS = [
    (0, 0, 0),
    (1, 0, 0),
    (-1, 0, 0),
    (0, 1, 0),
    (0, -1, 0),
    (0, 0, 1),
    (0, 0, -1),
    (1, 1, 0),
    (-1, -1, 0),
    (1, -1, 0),
    (-1, 1, 0),
    (1, 0, 1),
    (-1, 0, -1),
    (1, 0, -1),
    (-1, 0, 1),
    (0, 1, 1),
    (0, -1, -1),
    (0, 1, -1),
    (0, -1, 1),
]
WEIGHTS = [1.0 / 3.0] + [1.0 / 18.0] * 6 + [1.0 / 36.0] * 12
KAPPA = 4.0
RELAX = 0.9
UP = [i for i in range(19) if DIRS[i][0] == 1]
DOWN = [i for i in range(19) if DIRS[i][0] == -1]

CX = 4
ROWS = 16
HALO = 8
EXT = ROWS + 2 * HALO
NZ = 128
TRIM = 4
INNER = EXT - 2 * TRIM
MARKERS = 2048
VEL, FULL = 3, 5
AT_VEL, AT_PLANE = 8, 48
SENT_ROWS = AT_PLANE + 20 * CX * FULL + 8
KX, FORCE, STATE = 8, 12, 15
KY, KZ, WORK = 4, 8, 12
INSIDE, OUTSIDE = (1, 2), (0, 3)
LANES = 128
F32 = jnp.float32
BF16 = jnp.bfloat16


def split(value):
    high = value.astype(BF16)
    low = (value - high.astype(F32)).astype(BF16)
    return high, low


def moments_of(values):
    density = functools.reduce(lambda a, b: a + b, values)
    inverse = 1.0 / density
    velocity = []
    for axis in range(3):
        plus = functools.reduce(lambda a, b: a + b, [values[i] for i in range(19) if DIRS[i][axis] == 1])
        minus = functools.reduce(lambda a, b: a + b, [values[i] for i in range(19) if DIRS[i][axis] == -1])
        velocity.append((plus - minus) * inverse)
    return density, velocity


def along(index, vectors):
    total = None
    for axis in range(3):
        sign = DIRS[index][axis]
        if sign == 0:
            continue
        if total is None:
            total = vectors[axis] if sign == 1 else -vectors[axis]
        else:
            total = total + vectors[axis] if sign == 1 else total - vectors[axis]
    return total


def relaxed(values, density, velocity, fluid, put, indices=range(19)):
    keep, rate = 1.0 - 1.0 / RELAX, 1.0 / RELAX
    scaled = density * rate
    base = scaled - 1.5 * scaled * (
        velocity[0] * velocity[0] + velocity[1] * velocity[1] + velocity[2] * velocity[2]
    )
    if 0 in indices:
        put(0, jnp.where(fluid, keep * values[0] + WEIGHTS[0] * base, values[0]))
    for index in range(1, 19, 2):
        if index not in indices:
            continue
        weight = WEIGHTS[index]
        first, second = values[index], values[index + 1]
        proj = along(index, velocity)
        scaled_proj = scaled * proj
        even = weight * (base + 4.5 * scaled_proj * proj)
        odd = (3.0 * weight) * scaled_proj
        put(index, jnp.where(fluid, keep * first + (even + odd), second))
        put(index + 1, jnp.where(fluid, keep * second + (even - odd), first))


def forced(base, force, put, indices=range(19)):
    if 0 in indices:
        put(0, base(0))
    for index in range(1, 19, 2):
        if index not in indices:
            continue
        push = (3.0 * WEIGHTS[index]) * along(index, force)
        put(index, base(index) + push)
        put(index + 1, base(index + 1) - push)


def interpolated(velocity, zcat, cols):
    z_high, z_low = zcat[0:NZ, cols], zcat[NZ : 2 * NZ, cols]
    return jnp.dot(velocity, jnp.concatenate([z_high, z_high, z_low], 0), preferred_element_type=F32)


def tripled(velocity):
    high, low = split(velocity)
    return jnp.concatenate([high, low, high], 1)


def averaged(found, y_rows, kx):
    rows = y_rows.shape[0]
    total = None
    for p, weight in enumerate(kx):
        product = found[p * rows : (p + 1) * rows] * y_rows
        part = sum(product[t * 8 + 8 : t * 8 + 16] for t in range(rows // 8 - 1)) + product[0:8]
        total = part * weight if total is None else total + part * weight
    return jnp.sum(total, axis=0, keepdims=True)


def weigh(weighted, ys, forces, state, planes, rows):
    for tile in range(16):
        cols = slice(tile * LANES, (tile + 1) * LANES)
        y_rows = ys[:, cols]
        for axis in range(3):
            for p, x in enumerate(planes):
                scale = forces(axis, tile) * state[KX + x, tile : tile + 1]
                at = (axis * 2 + p) * rows
                high, low = split(y_rows * scale)
                weighted[at : at + rows, cols] = high
                weighted[6 * rows + at : 6 * rows + at + rows, cols] = low


def contract(weighted, zcat):
    return lax.dot_general(weighted, zcat, (((1,), (1,)), ((), ())), preferred_element_type=F32)


def spread_at(spread, p, tile, rows, fluid):
    result = []
    for axis in range(3):
        at = (axis * 2 + p) * rows + tile * 8
        low = 6 * rows + at
        whole = spread[at : at + 8, 0:NZ] + spread[at : at + 8, NZ : 2 * NZ]
        result.append((whole + spread[low : low + 8, 0:NZ]) * fluid)
    return result


def moved(block, index, offset):
    _, shift_y, shift_z = DIRS[index]
    shift_y = (shift_y - offset) % block.shape[0]
    if shift_y:
        block = pltpu.roll(block, shift_y, 0)
    if shift_z:
        block = pltpu.roll(block, shift_z % NZ, 1)
    return block


def pack_kernel(own, solid, corner, frac, target, stiffness, disp, sent, cells, bottom, top, block, walls, blocks, *held):
    sems = held[-1]
    held = held[:-1]
    small = [
        pltpu.make_async_copy(source, target_ref, sems.at[k])
        for k, (source, target_ref) in enumerate(zip((corner, frac, target, stiffness, disp), held))
    ]
    large = [
        pltpu.make_async_copy(solid, walls, sems.at[5]),
        pltpu.make_async_copy(own, cells.at[0:19], sems.at[6]),
    ]
    for copy in small + large:
        copy.start()
    for copy in small:
        copy.wait()
    corner, frac, target, stiffness, disp = held
    values = [corner[1:2].astype(F32), corner[2:3].astype(F32), frac[0:1], frac[1:2], frac[2:3], stiffness[...]]
    values += [target[axis : axis + 1] for axis in range(3)] + [disp[axis : axis + 1] for axis in range(3)]
    for r, value in enumerate(values):
        block[r // 2 : r // 2 + 1, 64 * (r % 2) : 64 * (r % 2) + 64] = value
    whole = block[0:6]
    peers = sent.shape[0]
    period = float(peers * ROWS)
    first = (lax.broadcasted_iota(jnp.int32, (6, LANES), 0) == 0) & (
        lax.broadcasted_iota(jnp.int32, (6, LANES), 1) < 64
    )
    for peer in range(peers):
        away = whole - float(peer * ROWS)
        away = away - jnp.where(away >= period / 2, period, jnp.where(away < -period / 2, -period, 0.0))
        adjusted = jnp.where(first, away, whole)
        for pair in range(3):
            blocks[peer, pair] = adjusted[2 * pair : 2 * pair + 2]
    going = pltpu.make_async_copy(blocks, sent, sems.at[7])
    going.start()
    for copy in large:
        copy.wait()
    for buffer in (bottom, top):
        for at in (0, AT_PLANE - 8, SENT_ROWS - 8):
            buffer[at : at + 8] = jnp.zeros((8, NZ), F32)
    for x in range(CX):
        cells[19, x] = walls[x].astype(F32)
        for buffer, rows, full, vel in ((bottom, slice(8, 16), 3, 0), (top, slice(0, 8), 0, 5)):
            values = [cells[i, x, rows] for i in range(20)]
            for i, value in enumerate(values):
                at = AT_PLANE + (i * CX + x) * FULL
                buffer[at : at + FULL] = value[full : full + FULL]
            for axis, value in enumerate(moments_of(values[0:19])[1]):
                at = AT_VEL + (axis * CX + x) * VEL
                buffer[at : at + VEL] = value[vel : vel + VEL]
    going.wait()


def own_kernel(cells, vcat, base, walls):
    for x in range(CX):
        walls[x] = cells[19, x]
        values = [cells[i, x] for i in range(19)]
        density, velocity = moments_of(values)
        for axis in range(3):
            at = (axis * CX + x) * ROWS
            vcat[at : at + ROWS, 0:NZ], vcat[at : at + ROWS, NZ:] = split(velocity[axis])

        def put(i, value):
            base[i, x] = value

        relaxed(values, density, velocity, cells[19, x] < 0.5, put)


def outer_kernel(low, walls, high, vcat, base, fluid, fluid_inner):
    row = lax.broadcasted_iota(jnp.int32, (16, NZ), 0)
    received = (row < VEL) | (row >= HALO + FULL)
    for x in range(CX):

        def pop(i):
            at = AT_PLANE + (i * CX + x) * FULL
            return jnp.concatenate([low[at - VEL : at - VEL + 8], high[at : at + 8]], 0)

        wall = pop(19)
        is_fluid = 1.0 - jnp.concatenate([wall[0:8], walls[x], wall[8:16]], 0)
        fluid[x] = is_fluid
        fluid_inner[x] = pltpu.roll(is_fluid, EXT - TRIM, 0)[0:INNER]
        values = [pop(i) for i in range(19)]
        density, velocity = moments_of(values)
        for axis in range(3):
            at = AT_VEL + (axis * CX + x) * VEL
            sent = jnp.concatenate([low[at : at + 8], high[at - FULL : at - FULL + 8]], 0)
            known = jnp.where(received, sent, velocity[axis])
            at = (axis * CX + x) * ROWS
            vcat[at : at + ROWS, 0:NZ], vcat[at : at + ROWS, NZ:] = split(known)

        def put(i, value):
            base[i, x] = value

        relaxed(values, density, velocity, wall < 0.5, put)


def dense(cells, first, weights):
    offset = cells - first
    value = jnp.where(offset == 3.0, weights[3], 0.0)
    for k in (2, 1, 0):
        value = jnp.where(offset == float(k), weights[k], value)
    return value


def kernel_weights(frac):
    root = jnp.sqrt(1.0 + 4.0 * frac - 4.0 * frac * frac)
    second = (3.0 - 2.0 * frac + root) / 8.0
    third = (1.0 + 2.0 * frac + root) / 8.0
    return [0.5 - third, second, third, 0.5 - second]


def weights_kernel(markers, zcat, ys, state, work):
    left = lax.broadcasted_iota(jnp.int32, (2, LANES), 1) < 64
    for tile in range(16):
        even, odd = [], []
        for pair in range(3):
            one, two = markers[2 * tile, pair], markers[2 * tile + 1, pair]
            evens = jnp.where(left, one, pltpu.roll(two, 64, 1))
            odds = jnp.where(left, pltpu.roll(one, 64, 1), two)
            even += [evens[0:1], evens[1:2]]
            odd += [odds[0:1], odds[1:2]]
        kept = (even[3], odd[3], even[4], odd[2], odd[4], even[5], odd[5], even[0])
        for r, value in enumerate(kept):
            state[r, tile : tile + 1] = value
        for r, value in enumerate((odd[0], even[1], odd[1], even[2])):
            work[r, tile : tile + 1] = value
    for r, target, at in ((1, state, KX), (2, work, KY), (3, work, KZ)):
        for k, value in enumerate(kernel_weights(work[r])):
            target[at + k] = value

    z_cell = lax.broadcasted_iota(jnp.int32, (NZ, LANES), 0).astype(F32)
    y_cell = lax.broadcasted_iota(jnp.int32, (EXT, LANES), 0).astype(F32) - HALO
    for tile in range(16):
        cols = slice(tile * LANES, (tile + 1) * LANES)

        def row(r):
            return work[r, tile : tile + 1]

        zcat[0:NZ, cols], zcat[NZ : 2 * NZ, cols] = split(dense(z_cell, row(0), [row(KZ + k) for k in range(4)]))
        ys[:, cols] = dense(y_cell, state[7, tile : tile + 1], [row(KY + k) for k in range(4)])


def first_kernel(
    vown, vouter, own, outer, fluid, zcat, ys, given, up, down, push, state, work, weighted, spread
):
    state[0:FORCE] = given[...]
    velocity = jnp.concatenate([vown[...], vouter[...]], 0)
    velocity = jnp.concatenate([velocity, velocity[:, 0:NZ]], 1)
    for pair in range(8):
        found = interpolated(velocity, zcat, slice(pair * 256, (pair + 1) * 256))
        for half in range(2):
            tile = 2 * pair + half
            for axis in range(3):
                at, lanes = axis * CX * ROWS, slice(half * LANES, (half + 1) * LANES)
                cols = slice(tile * LANES, (tile + 1) * LANES)
                kx = [state[KX + x, tile : tile + 1] for x in range(CX)]
                inner = averaged(found[at : at + CX * ROWS, lanes], ys[HALO : HALO + ROWS, cols], kx)
                y_outer = jnp.concatenate([ys[0:HALO, cols], ys[HALO + ROWS :, cols]], 0)
                at += 3 * CX * ROWS
                work[axis, tile : tile + 1] = inner + averaged(found[at : at + CX * ROWS, lanes], y_outer, kx)
    for axis in range(3):
        mean, disp = work[axis], state[4 + axis]
        state[FORCE + axis] = KAPPA * (state[axis] - mean) - state[3] * disp
        state[4 + axis] = disp + mean

    weigh(weighted, ys, lambda axis, tile: state[FORCE + axis, tile : tile + 1], state, OUTSIDE, EXT)
    spread[...] = contract(weighted[...], zcat[...])
    for p, x in enumerate(OUTSIDE):
        for tile in range(4):
            rows = slice(tile * 8, tile * 8 + 8)
            for axis, value in enumerate(spread_at(spread, p, tile, EXT, fluid[x, rows])):
                push[axis, p, rows] = value
    for p, faces, target in ((1, UP, up), (0, DOWN, down)):
        for j, index in enumerate(faces):
            force = along(index, [push[axis, p] for axis in range(3)])
            x = OUTSIDE[p]
            plane = jnp.concatenate([outer[index, x, 0:HALO], own[index, x], outer[index, x, HALO:]], 0)
            plane = plane + (3.0 * WEIGHTS[index]) * force
            target[j] = moved(plane, index, TRIM)[0:INNER]


def inner_kernel(
    own, outer, fluid, fluid_inner, push, ys, zcat, state, edge, found, inside, trimmed, post, moving, velocities, weighted, spread
):
    trimmed[...] = ys[TRIM : TRIM + INNER]
    weigh(weighted, ys, lambda axis, tile: state[FORCE + axis, tile : tile + 1], state, INSIDE, EXT)
    spread[...] = contract(weighted[...], zcat[...])
    for x in range(CX):
        for tile in range(4):
            rows = slice(tile * 8, tile * 8 + 8)

            def put(i, value):
                post[i, x, rows] = value

            if x in INSIDE:
                force = spread_at(spread, x - 1, tile, EXT, fluid[x, rows])
            else:
                force = [push[axis, x // 3, rows] for axis in range(3)]

            def base(i):
                if tile in (0, 3):
                    return outer[i, x, 0:8] if tile == 0 else outer[i, x, 8:16]
                return own[i, x, tile * 8 - 8 : tile * 8]

            forced(base, force, put)
    for index in range(19):
        for x in range(CX):
            source = x - DIRS[index][0]
            if not 0 <= source < CX:
                continue
            plane = moved(post[index, source], index, TRIM)[0:INNER]
            if x in INSIDE:
                moving[index, x - 1] = plane
            else:
                edge[index, x // 3] = plane
    for p, x in enumerate(INSIDE):
        for tile in range(3):
            rows = slice(tile * 8, tile * 8 + 8)
            values = [moving[i, p, rows] for i in range(19)]
            density, velocity = moments_of(values)
            for axis in range(3):
                at = (axis * 2 + p) * INNER + tile * 8
                velocities[at : at + 8] = velocity[axis]

            def put(i, value):
                inside[i, p, rows] = value

            relaxed(values, density, velocity, fluid_inner[x, rows] > 0.5, put)
    partial_means(velocities, zcat, trimmed, state, INSIDE, lambda axis, tile, value: found.__setitem__((axis, slice(tile, tile + 1)), value))


def partial_means(velocities, zcat, ys, state, planes, put):
    velocity = tripled(velocities[...])
    for pair in range(8):
        found = interpolated(velocity, zcat, slice(pair * 256, (pair + 1) * 256))
        for half in range(2):
            tile = 2 * pair + half
            y_rows = ys[:, tile * LANES : (tile + 1) * LANES]
            for axis in range(3):
                at = axis * 2 * INNER
                part = averaged(
                    found[at : at + 2 * INNER, half * LANES : (half + 1) * LANES],
                    y_rows,
                    [state[KX + x, tile : tile + 1] for x in planes],
                )
                put(axis, tile, part)


def edge_values(edge, up, down, x, rows):
    def value(i):
        if x == 0 and DIRS[i][0] == 1:
            return up[UP.index(i), rows]
        if x == CX - 1 and DIRS[i][0] == -1:
            return down[DOWN.index(i), rows]
        return edge[i, x // 3, rows]

    return [value(i) for i in range(19)]


def second_kernel(edge, up, down, ys, zcat, state, found, force, density, velocities, back, mean, rest):
    for p, x in enumerate(OUTSIDE):
        for tile in range(3):
            rows = slice(tile * 8, tile * 8 + 8)
            dense_at, velocity = moments_of(edge_values(edge, up, down, x, rows))
            density[p, rows] = dense_at
            for axis in range(3):
                at = (axis * 2 + p) * INNER + tile * 8
                velocities[at : at + 8] = velocity[axis]
    partial_means(velocities, zcat, ys, state, OUTSIDE, lambda axis, tile, value: mean.__setitem__((axis, slice(tile, tile + 1)), value))
    mine = (state[7] >= 0.0) & (state[7] < float(ROWS))
    moved_to, pulls = [], []
    for axis in range(3):
        average = found[axis] + mean[axis]
        disp = state[4 + axis]
        pull = KAPPA * (state[axis] - average) - state[3] * disp
        force[axis] = pull
        moved_to.append(jnp.where(mine, disp + average, 0.0))
        pulls.append(jnp.where(mine, pull, 0.0))
    values = moved_to + pulls
    left = lax.broadcasted_iota(jnp.int32, (16, LANES), 1) < 64
    for r in range(3):
        even, odd = values[2 * r], values[2 * r + 1]
        rest[0, r] = jnp.where(left, even, pltpu.roll(odd, 64, 1))
        rest[1, r] = jnp.where(left, pltpu.roll(even, 64, 1), odd)
        for tile in range(16):
            back[2 * tile, r] = rest[0, r, tile : tile + 1]
            back[2 * tile + 1, r] = rest[1, r, tile : tile + 1]


def third_kernel(
    edge, up, down, fluid, density, velocities, force, ys, zcat, state, out_up, out_down, post, weighted, spread
):
    weigh(weighted, ys, lambda axis, tile: force[axis, tile : tile + 1], state, OUTSIDE, INNER)
    spread[...] = contract(weighted[...], zcat[...])
    for p, x in enumerate(OUTSIDE):
        for tile in range(3):
            rows = slice(tile * 8, tile * 8 + 8)

            def put(i, value):
                post[i, p, rows] = value

            values = edge_values(edge, up, down, x, rows)
            velocity = [velocities[pl.ds((axis * 2 + p) * INNER + tile * 8, 8)] for axis in range(3)]
            is_fluid = fluid[x, rows]
            relaxed(values, density[p, rows], velocity, is_fluid > 0.5, put)
            pushed = spread_at(spread, p, tile, INNER, is_fluid)
            forced(lambda i: post[i, p, rows], pushed, put)
    for j, index in enumerate(UP):
        out_up[j] = moved(post[index, 1], index, HALO - TRIM)[0:ROWS]
    for j, index in enumerate(DOWN):
        out_down[j] = moved(post[index, 0], index, HALO - TRIM)[0:ROWS]


def stream_kernel(inside, outside, fluid, force, ys, zcat, state, out, post, weighted, spread):
    weigh(weighted, ys, lambda axis, tile: force[axis, tile : tile + 1], state, INSIDE, INNER)
    spread[...] = contract(weighted[...], zcat[...])
    for p, x in enumerate(INSIDE):
        for tile in range(3):
            rows = slice(tile * 8, tile * 8 + 8)

            def put(i, value):
                post[i, p, rows] = value

            forced(lambda i: inside[i, p, rows], spread_at(spread, p, tile, INNER, fluid[x, rows]), put)
    for index in range(19):
        for x in range(CX):
            source = x - DIRS[index][0]
            if 0 <= source < CX:
                plane = post[index, source - 1] if source in INSIDE else outside[index, source // 3]
                out[index, x] = moved(plane, index, HALO - TRIM)[0:ROWS]
            else:
                out[index, x] = jnp.zeros((ROWS, NZ), F32)


def fill_kernel(part, up, down, out, sems):
    copies = []
    for j, index in enumerate(UP):
        copies.append(pltpu.make_async_copy(up.at[j], out.at[index, 0], sems.at[j]))
    for j, index in enumerate(DOWN):
        copies.append(pltpu.make_async_copy(down.at[j], out.at[index, CX - 1], sems.at[5 + j]))
    for copy in copies:
        copy.start()
    for copy in copies:
        copy.wait()


IN_VMEM = pl.BlockSpec(memory_space=pltpu.VMEM)
ANYWHERE = pl.BlockSpec(memory_space=pl.ANY)


def near(x):
    return pltpu.with_memory_space_constraint(x, pltpu.VMEM)


def run(kernel, args, outs, scratch=(), cost=4_000_000):
    return pl.pallas_call(
        kernel,
        out_shape=outs,
        in_specs=[IN_VMEM] * len(args),
        out_specs=jax.tree.map(lambda _: IN_VMEM, outs, is_leaf=lambda leaf: not isinstance(leaf, tuple)),
        scratch_shapes=list(scratch),
        compiler_params=pltpu.CompilerParams(vmem_limit_bytes=24 * 2**20),
        cost_estimate=pl.CostEstimate(flops=0, transcendentals=0, bytes_accessed=cost),
    )(*args)


def ring(axis):
    peers = lax.axis_size(axis)
    forward = [(i, (i + 1) % peers) for i in range(peers)]
    return forward, [(j, i) for i, j in forward]


def parts(populations, solid, marker_corner, marker_frac, marker_target, stiffness, displacement):
    peers = lax.axis_size("sub")
    sub_up, sub_down = ring("sub")
    plate_up, plate_down = ring("plate")
    args = (populations, solid, marker_corner, marker_frac, marker_target, stiffness.reshape(1, 64), displacement)
    shape = (SENT_ROWS, NZ)
    sent, cells, bottom, top = pl.pallas_call(
        pack_kernel,
        out_shape=(
            jax.ShapeDtypeStruct((peers, 3, 2, LANES), F32),
            pltpu.VMEM((20, CX, ROWS, NZ), F32),
            pltpu.VMEM(shape, F32),
            pltpu.VMEM(shape, F32),
        ),
        in_specs=[pl.BlockSpec(memory_space=pltpu.HBM)] * 7,
        out_specs=[pl.BlockSpec(memory_space=pltpu.HBM), *[IN_VMEM] * 3],
        scratch_shapes=[
            pltpu.VMEM((8, LANES), F32),
            pltpu.VMEM(solid.shape, jnp.int32),
            pltpu.VMEM((peers, 3, 2, LANES), F32),
            *[pltpu.VMEM(arg.shape, arg.dtype) for arg in args[2:]],
            pltpu.SemaphoreType.DMA((8,)),
        ],
        compiler_params=pltpu.CompilerParams(vmem_limit_bytes=8 * 2**20),
        name="pack_kernel",
    )(*[pltpu.with_memory_space_constraint(arg, pltpu.HBM) for arg in args])
    markers = lax.all_to_all(sent, "sub", 0, 0, tiled=True)
    low = lax.ppermute(bottom, "sub", sub_up)
    high = lax.ppermute(top, "sub", sub_down)
    zcat, ys, given = run(
        weights_kernel,
        (near(markers),),
        (
            pltpu.VMEM((2 * NZ, MARKERS), BF16),
            pltpu.VMEM((EXT, MARKERS), F32),
            pltpu.VMEM((FORCE, 16, LANES), F32),
        ),
        (pltpu.VMEM((WORK, 16, LANES), F32),),
    )
    half = (pltpu.VMEM((3 * CX * ROWS, 2 * NZ), BF16), pltpu.VMEM((19, CX, ROWS, NZ), F32))
    vown, own, walls = run(own_kernel, (near(cells),), (*half, pltpu.VMEM((CX, ROWS, NZ), F32)))
    vouter, outer, fluid, fluid_inner = run(
        outer_kernel,
        (near(low), near(walls), near(high)),
        (*half, pltpu.VMEM((CX, EXT, NZ), F32), pltpu.VMEM((CX, INNER, NZ), F32)),
    )
    faces = (pltpu.VMEM((5, INNER, NZ), F32),) * 2
    plane_pairs = pltpu.VMEM((19, 2, INNER, NZ), F32)
    rows = pltpu.VMEM((3, 16, LANES), F32)

    def spreading(cells):
        return (pltpu.VMEM((12 * cells, MARKERS), BF16), pltpu.VMEM((12 * cells, 2 * NZ), F32))

    up, down, push, state = run(
        first_kernel,
        (near(vown), near(vouter), near(own), near(outer), near(fluid), near(zcat), near(ys), near(given)),
        (*faces, pltpu.VMEM((3, 2, EXT, NZ), F32), pltpu.VMEM((STATE, 16, LANES), F32)),
        (rows, *spreading(EXT)),
    )
    up = lax.ppermute(up, "plate", plate_up)
    down = lax.ppermute(down, "plate", plate_down)
    known = (near(ys), near(zcat), near(state))
    trimmed = pltpu.VMEM((INNER, MARKERS), F32)
    edge, found, inside, ys = run(
        inner_kernel,
        (near(own), near(outer), near(fluid), near(fluid_inner), near(push), *known),
        (plane_pairs, rows, pltpu.HBM((19, 2, INNER, NZ), F32), trimmed),
        (
            pltpu.VMEM((19, CX, EXT, NZ), F32),
            plane_pairs,
            pltpu.VMEM((6 * INNER, NZ), F32),
            *spreading(EXT),
        ),
        cost=12_000_000,
    )
    known = (near(ys), near(zcat), near(state))
    edges = (near(edge), near(up), near(down))
    force, density, velocities, back = run(
        second_kernel,
        (*edges, *known, near(found)),
        (
            rows,
            pltpu.VMEM((2, INNER, NZ), F32),
            pltpu.VMEM((6 * INNER, NZ), F32),
            jax.ShapeDtypeStruct((peers, 3, 1, LANES), F32),
        ),
        (rows, pltpu.VMEM((2, 3, 16, LANES), F32)),
    )
    back = lax.all_to_all(back, "sub", 0, 0, tiled=True)
    up, down, outside = run(
        third_kernel,
        (*edges, near(fluid_inner), near(density), near(velocities), near(force), *known),
        (*[pltpu.VMEM((5, ROWS, NZ), F32)] * 2, plane_pairs),
        spreading(INNER),
    )
    up = lax.ppermute(up, "plate", plate_up)
    down = lax.ppermute(down, "plate", plate_down)
    part = run(
        stream_kernel,
        (pltpu.with_memory_space_constraint(inside, pltpu.HBM), near(outside), near(fluid_inner), near(force), *known),
        jax.ShapeDtypeStruct((19, CX, ROWS, NZ), F32),
        (plane_pairs, *spreading(INNER)),
        cost=12_000_000,
    )
    out = pl.pallas_call(
        fill_kernel,
        out_shape=jax.ShapeDtypeStruct((19, CX, ROWS, NZ), F32),
        in_specs=[ANYWHERE, IN_VMEM, IN_VMEM],
        out_specs=ANYWHERE,
        scratch_shapes=[pltpu.SemaphoreType.DMA((10,))],
        input_output_aliases={0: 0},
        compiler_params=pltpu.CompilerParams(vmem_limit_bytes=8 * 2**20),
        name="fill_kernel",
    )(part, near(up), near(down))
    result = jnp.sum(back, 0).reshape(6, 64)
    return (out, result[:3], result[3:])


def solution(mesh):
    in_specs = (
        P(None, "plate", "sub", None),
        P("plate", "sub", None),
        P(None, ("plate", "sub")),
        P(None, ("plate", "sub")),
        P(None, ("plate", "sub")),
        P(("plate", "sub")),
        P(None, ("plate", "sub")),
    )
    out_specs = (
        P(None, "plate", "sub", None),
        P(None, ("plate", "sub")),
        P(None, ("plate", "sub")),
    )
    return jax.shard_map(parts, mesh=mesh, in_specs=in_specs, out_specs=out_specs, check_vma=False)
```

```python
import functools
import jax
import jax.numpy as jnp
from jax import lax
from jax.experimental import pallas as pl
from jax.experimental.pallas import tpu as pltpu
from jax.sharding import PartitionSpec as P

DIRS = [
    (0, 0, 0),
    (1, 0, 0),
    (-1, 0, 0),
    (0, 1, 0),
    (0, -1, 0),
    (0, 0, 1),
    (0, 0, -1),
    (1, 1, 0),
    (-1, -1, 0),
    (1, -1, 0),
    (-1, 1, 0),
    (1, 0, 1),
    (-1, 0, -1),
    (1, 0, -1),
    (-1, 0, 1),
    (0, 1, 1),
    (0, -1, -1),
    (0, 1, -1),
    (0, -1, 1),
]
WEIGHTS = [1.0 / 3.0] + [1.0 / 18.0] * 6 + [1.0 / 36.0] * 12
KAPPA = 4.0
RELAX = 0.9
UP = [i for i in range(19) if DIRS[i][0] == 1]
DOWN = [i for i in range(19) if DIRS[i][0] == -1]

CX = 4
ROWS = 16
HALO = 8
EXT = ROWS + 2 * HALO
NZ = 128
TRIM = 4
INNER = EXT - 2 * TRIM
MARKERS = 2048
VEL, FULL = 3, 5
AT_VEL, AT_PLANE = 8, 48
SENT_ROWS = AT_PLANE + 20 * CX * FULL + 8
KX, FORCE, STATE = 8, 12, 15
KY, KZ, WORK = 4, 8, 12
INSIDE, OUTSIDE = (1, 2), (0, 3)
LANES = 128
F32 = jnp.float32
BF16 = jnp.bfloat16


def split(value):
    high = value.astype(BF16)
    low = (value - high.astype(F32)).astype(BF16)
    return high, low


def moments_of(values):
    density = functools.reduce(lambda a, b: a + b, values)
    inverse = 1.0 / density
    velocity = []
    for axis in range(3):
        plus = functools.reduce(lambda a, b: a + b, [values[i] for i in range(19) if DIRS[i][axis] == 1])
        minus = functools.reduce(lambda a, b: a + b, [values[i] for i in range(19) if DIRS[i][axis] == -1])
        velocity.append((plus - minus) * inverse)
    return density, velocity


def along(index, vectors):
    total = None
    for axis in range(3):
        sign = DIRS[index][axis]
        if sign == 0:
            continue
        if total is None:
            total = vectors[axis] if sign == 1 else -vectors[axis]
        else:
            total = total + vectors[axis] if sign == 1 else total - vectors[axis]
    return total


def relaxed(values, density, velocity, fluid, put, indices=range(19)):
    keep, rate = 1.0 - 1.0 / RELAX, 1.0 / RELAX
    scaled = density * rate
    base = scaled - 1.5 * scaled * (
        velocity[0] * velocity[0] + velocity[1] * velocity[1] + velocity[2] * velocity[2]
    )
    if 0 in indices:
        put(0, jnp.where(fluid, keep * values[0] + WEIGHTS[0] * base, values[0]))
    for index in range(1, 19, 2):
        if index not in indices:
            continue
        weight = WEIGHTS[index]
        first, second = values[index], values[index + 1]
        proj = along(index, velocity)
        scaled_proj = scaled * proj
        even = weight * (base + 4.5 * scaled_proj * proj)
        odd = (3.0 * weight) * scaled_proj
        put(index, jnp.where(fluid, keep * first + (even + odd), second))
        put(index + 1, jnp.where(fluid, keep * second + (even - odd), first))


def forced(base, force, put, indices=range(19)):
    if 0 in indices:
        put(0, base(0))
    for index in range(1, 19, 2):
        if index not in indices:
            continue
        push = (3.0 * WEIGHTS[index]) * along(index, force)
        put(index, base(index) + push)
        put(index + 1, base(index + 1) - push)


def interpolated(velocity, zcat, cols):
    z_high, z_low = zcat[0:NZ, cols], zcat[NZ : 2 * NZ, cols]
    return jnp.dot(velocity, jnp.concatenate([z_high, z_high, z_low], 0), preferred_element_type=F32)


def tripled(velocity):
    high, low = split(velocity)
    return jnp.concatenate([high, low, high], 1)


def averaged(found, y_rows, kx):
    rows = y_rows.shape[0]
    total = None
    for p, weight in enumerate(kx):
        product = found[p * rows : (p + 1) * rows] * y_rows
        part = sum(product[t * 8 + 8 : t * 8 + 16] for t in range(rows // 8 - 1)) + product[0:8]
        total = part * weight if total is None else total + part * weight
    return jnp.sum(total, axis=0, keepdims=True)


def weigh(weighted, ys, forces, state, planes, rows):
    for tile in range(16):
        cols = slice(tile * LANES, (tile + 1) * LANES)
        y_rows = ys[:, cols]
        for axis in range(3):
            for p, x in enumerate(planes):
                scale = forces(axis, tile) * state[KX + x, tile : tile + 1]
                at = (axis * 2 + p) * rows
                high, low = split(y_rows * scale)
                weighted[at : at + rows, cols] = high
                weighted[6 * rows + at : 6 * rows + at + rows, cols] = low


def contract(weighted, zcat):
    return lax.dot_general(weighted, zcat, (((1,), (1,)), ((), ())), preferred_element_type=F32)


def spread_at(spread, p, tile, rows, fluid):
    result = []
    for axis in range(3):
        at = (axis * 2 + p) * rows + tile * 8
        low = 6 * rows + at
        whole = spread[at : at + 8, 0:NZ] + spread[at : at + 8, NZ : 2 * NZ]
        result.append((whole + spread[low : low + 8, 0:NZ]) * fluid)
    return result


def moved(block, index, offset):
    _, shift_y, shift_z = DIRS[index]
    shift_y = (shift_y - offset) % block.shape[0]
    if shift_y:
        block = pltpu.roll(block, shift_y, 0)
    if shift_z:
        block = pltpu.roll(block, shift_z % NZ, 1)
    return block


def pack_kernel(own, solid, corner, frac, target, stiffness, disp, sent, cells, bottom, top, block, walls, blocks, *held):
    sems = held[-1]
    held = held[:-1]
    small = [
        pltpu.make_async_copy(source, target_ref, sems.at[k])
        for k, (source, target_ref) in enumerate(zip((corner, frac, target, stiffness, disp), held))
    ]
    large = [
        pltpu.make_async_copy(solid, walls, sems.at[5]),
        pltpu.make_async_copy(own, cells.at[0:19], sems.at[6]),
    ]
    for copy in small + large:
        copy.start()
    for copy in small:
        copy.wait()
    corner, frac, target, stiffness, disp = held
    values = [corner[1:2].astype(F32), corner[2:3].astype(F32), frac[0:1], frac[1:2], frac[2:3], stiffness[...]]
    values += [target[axis : axis + 1] for axis in range(3)] + [disp[axis : axis + 1] for axis in range(3)]
    for r, value in enumerate(values):
        block[r // 2 : r // 2 + 1, 64 * (r % 2) : 64 * (r % 2) + 64] = value
    whole = block[0:6]
    peers = sent.shape[0]
    period = float(peers * ROWS)
    first = (lax.broadcasted_iota(jnp.int32, (6, LANES), 0) == 0) & (
        lax.broadcasted_iota(jnp.int32, (6, LANES), 1) < 64
    )
    for peer in range(peers):
        away = whole - float(peer * ROWS)
        away = away - jnp.where(away >= period / 2, period, jnp.where(away < -period / 2, -period, 0.0))
        adjusted = jnp.where(first, away, whole)
        for pair in range(3):
            blocks[peer, pair] = adjusted[2 * pair : 2 * pair + 2]
    going = pltpu.make_async_copy(blocks, sent, sems.at[7])
    going.start()
    for copy in large:
        copy.wait()
    for buffer in (bottom, top):
        for at in (0, AT_PLANE - 8, SENT_ROWS - 8):
            buffer[at : at + 8] = jnp.zeros((8, NZ), F32)
    for x in range(CX):
        cells[19, x] = walls[x].astype(F32)
        for buffer, rows, full, vel in ((bottom, slice(8, 16), 3, 0), (top, slice(0, 8), 0, 5)):
            values = [cells[i, x, rows] for i in range(20)]
            for i, value in enumerate(values):
                at = AT_PLANE + (i * CX + x) * FULL
                buffer[at : at + FULL] = value[full : full + FULL]
            for axis, value in enumerate(moments_of(values[0:19])[1]):
                at = AT_VEL + (axis * CX + x) * VEL
                buffer[at : at + VEL] = value[vel : vel + VEL]
    going.wait()


def own_kernel(cells, vcat, base, walls):
    for x in range(CX):
        walls[x] = cells[19, x]
        values = [cells[i, x] for i in range(19)]
        density, velocity = moments_of(values)
        for axis in range(3):
            at = (axis * CX + x) * ROWS
            vcat[at : at + ROWS, 0:NZ], vcat[at : at + ROWS, NZ:] = split(velocity[axis])

        def put(i, value):
            base[i, x] = value

        relaxed(values, density, velocity, cells[19, x] < 0.5, put)


def outer_kernel(low, walls, high, vcat, base, fluid, fluid_inner):
    row = lax.broadcasted_iota(jnp.int32, (16, NZ), 0)
    received = (row < VEL) | (row >= HALO + FULL)
    for x in range(CX):

        def pop(i):
            at = AT_PLANE + (i * CX + x) * FULL
            return jnp.concatenate([low[at - VEL : at - VEL + 8], high[at : at + 8]], 0)

        wall = pop(19)
        is_fluid = 1.0 - jnp.concatenate([wall[0:8], walls[x], wall[8:16]], 0)
        fluid[x] = is_fluid
        fluid_inner[x] = pltpu.roll(is_fluid, EXT - TRIM, 0)[0:INNER]
        values = [pop(i) for i in range(19)]
        density, velocity = moments_of(values)
        for axis in range(3):
            at = AT_VEL + (axis * CX + x) * VEL
            sent = jnp.concatenate([low[at : at + 8], high[at - FULL : at - FULL + 8]], 0)
            known = jnp.where(received, sent, velocity[axis])
            at = (axis * CX + x) * ROWS
            vcat[at : at + ROWS, 0:NZ], vcat[at : at + ROWS, NZ:] = split(known)

        def put(i, value):
            base[i, x] = value

        relaxed(values, density, velocity, wall < 0.5, put)


def dense(cells, first, weights):
    offset = cells - first
    value = jnp.where(offset == 3.0, weights[3], 0.0)
    for k in (2, 1, 0):
        value = jnp.where(offset == float(k), weights[k], value)
    return value


def kernel_weights(frac):
    root = jnp.sqrt(1.0 + 4.0 * frac - 4.0 * frac * frac)
    second = (3.0 - 2.0 * frac + root) / 8.0
    third = (1.0 + 2.0 * frac + root) / 8.0
    return [0.5 - third, second, third, 0.5 - second]


def weights_kernel(markers, zcat, ys, state, work):
    left = lax.broadcasted_iota(jnp.int32, (2, LANES), 1) < 64
    for tile in range(16):
        even, odd = [], []
        for pair in range(3):
            one, two = markers[2 * tile, pair], markers[2 * tile + 1, pair]
            evens = jnp.where(left, one, pltpu.roll(two, 64, 1))
            odds = jnp.where(left, pltpu.roll(one, 64, 1), two)
            even += [evens[0:1], evens[1:2]]
            odd += [odds[0:1], odds[1:2]]
        kept = (even[3], odd[3], even[4], odd[2], odd[4], even[5], odd[5], even[0])
        for r, value in enumerate(kept):
            state[r, tile : tile + 1] = value
        for r, value in enumerate((odd[0], even[1], odd[1], even[2])):
            work[r, tile : tile + 1] = value
    for r, target, at in ((1, state, KX), (2, work, KY), (3, work, KZ)):
        for k, value in enumerate(kernel_weights(work[r])):
            target[at + k] = value

    z_cell = lax.broadcasted_iota(jnp.int32, (NZ, LANES), 0).astype(F32)
    y_cell = lax.broadcasted_iota(jnp.int32, (EXT, LANES), 0).astype(F32) - HALO
    for tile in range(16):
        cols = slice(tile * LANES, (tile + 1) * LANES)

        def row(r):
            return work[r, tile : tile + 1]

        zcat[0:NZ, cols], zcat[NZ : 2 * NZ, cols] = split(dense(z_cell, row(0), [row(KZ + k) for k in range(4)]))
        ys[:, cols] = dense(y_cell, state[7, tile : tile + 1], [row(KY + k) for k in range(4)])


def first_kernel(
    vown, vouter, own, outer, fluid, zcat, ys, given, up, down, push, state, work, weighted, spread
):
    state[0:FORCE] = given[...]
    velocity = jnp.concatenate([vown[...], vouter[...]], 0)
    velocity = jnp.concatenate([velocity, velocity[:, 0:NZ]], 1)
    for pair in range(8):
        found = interpolated(velocity, zcat, slice(pair * 256, (pair + 1) * 256))
        for half in range(2):
            tile = 2 * pair + half
            for axis in range(3):
                at, lanes = axis * CX * ROWS, slice(half * LANES, (half + 1) * LANES)
                cols = slice(tile * LANES, (tile + 1) * LANES)
                kx = [state[KX + x, tile : tile + 1] for x in range(CX)]
                inner = averaged(found[at : at + CX * ROWS, lanes], ys[HALO : HALO + ROWS, cols], kx)
                y_outer = jnp.concatenate([ys[0:HALO, cols], ys[HALO + ROWS :, cols]], 0)
                at += 3 * CX * ROWS
                work[axis, tile : tile + 1] = inner + averaged(found[at : at + CX * ROWS, lanes], y_outer, kx)
    for axis in range(3):
        mean, disp = work[axis], state[4 + axis]
        state[FORCE + axis] = KAPPA * (state[axis] - mean) - state[3] * disp
        state[4 + axis] = disp + mean

    weigh(weighted, ys, lambda axis, tile: state[FORCE + axis, tile : tile + 1], state, OUTSIDE, EXT)
    spread[...] = contract(weighted[...], zcat[...])
    for p, x in enumerate(OUTSIDE):
        for tile in range(4):
            rows = slice(tile * 8, tile * 8 + 8)
            for axis, value in enumerate(spread_at(spread, p, tile, EXT, fluid[x, rows])):
                push[axis, p, rows] = value
    for p, faces, target in ((1, UP, up), (0, DOWN, down)):
        for j, index in enumerate(faces):
            force = along(index, [push[axis, p] for axis in range(3)])
            x = OUTSIDE[p]
            plane = jnp.concatenate([outer[index, x, 0:HALO], own[index, x], outer[index, x, HALO:]], 0)
            plane = plane + (3.0 * WEIGHTS[index]) * force
            target[j] = moved(plane, index, TRIM)[0:INNER]


def inner_kernel(
    own, outer, fluid, fluid_inner, push, ys, zcat, state, edge, found, inside, trimmed, post, moving, velocities, weighted, spread
):
    trimmed[...] = ys[TRIM : TRIM + INNER]
    weigh(weighted, ys, lambda axis, tile: state[FORCE + axis, tile : tile + 1], state, INSIDE, EXT)
    spread[...] = contract(weighted[...], zcat[...])
    for x in range(CX):
        for tile in range(4):
            rows = slice(tile * 8, tile * 8 + 8)

            def put(i, value):
                post[i, x, rows] = value

            if x in INSIDE:
                force = spread_at(spread, x - 1, tile, EXT, fluid[x, rows])
            else:
                force = [push[axis, x // 3, rows] for axis in range(3)]

            def base(i):
                if tile in (0, 3):
                    return outer[i, x, 0:8] if tile == 0 else outer[i, x, 8:16]
                return own[i, x, tile * 8 - 8 : tile * 8]

            forced(base, force, put)
    for index in range(19):
        for x in range(CX):
            source = x - DIRS[index][0]
            if not 0 <= source < CX:
                continue
            plane = moved(post[index, source], index, TRIM)[0:INNER]
            if x in INSIDE:
                moving[index, x - 1] = plane
            else:
                edge[index, x // 3] = plane
    for p, x in enumerate(INSIDE):
        for tile in range(3):
            rows = slice(tile * 8, tile * 8 + 8)
            values = [moving[i, p, rows] for i in range(19)]
            density, velocity = moments_of(values)
            for axis in range(3):
                at = (axis * 2 + p) * INNER + tile * 8
                velocities[at : at + 8] = velocity[axis]

            def put(i, value):
                inside[i, p, rows] = value

            relaxed(values, density, velocity, fluid_inner[x, rows] > 0.5, put)
    partial_means(velocities, zcat, trimmed, state, INSIDE, lambda axis, tile, value: found.__setitem__((axis, slice(tile, tile + 1)), value))


def partial_means(velocities, zcat, ys, state, planes, put):
    velocity = tripled(velocities[...])
    for pair in range(8):
        found = interpolated(velocity, zcat, slice(pair * 256, (pair + 1) * 256))
        for half in range(2):
            tile = 2 * pair + half
            y_rows = ys[:, tile * LANES : (tile + 1) * LANES]
            for axis in range(3):
                at = axis * 2 * INNER
                part = averaged(
                    found[at : at + 2 * INNER, half * LANES : (half + 1) * LANES],
                    y_rows,
                    [state[KX + x, tile : tile + 1] for x in planes],
                )
                put(axis, tile, part)


def edge_values(edge, up, down, x, rows):
    def value(i):
        if x == 0 and DIRS[i][0] == 1:
            return up[UP.index(i), rows]
        if x == CX - 1 and DIRS[i][0] == -1:
            return down[DOWN.index(i), rows]
        return edge[i, x // 3, rows]

    return [value(i) for i in range(19)]


def second_kernel(edge, up, down, ys, zcat, state, found, force, density, velocities, back, mean, rest):
    for p, x in enumerate(OUTSIDE):
        for tile in range(3):
            rows = slice(tile * 8, tile * 8 + 8)
            dense_at, velocity = moments_of(edge_values(edge, up, down, x, rows))
            density[p, rows] = dense_at
            for axis in range(3):
                at = (axis * 2 + p) * INNER + tile * 8
                velocities[at : at + 8] = velocity[axis]
    partial_means(velocities, zcat, ys, state, OUTSIDE, lambda axis, tile, value: mean.__setitem__((axis, slice(tile, tile + 1)), value))
    mine = (state[7] >= 0.0) & (state[7] < float(ROWS))
    moved_to, pulls = [], []
    for axis in range(3):
        average = found[axis] + mean[axis]
        disp = state[4 + axis]
        pull = KAPPA * (state[axis] - average) - state[3] * disp
        force[axis] = pull
        moved_to.append(jnp.where(mine, disp + average, 0.0))
        pulls.append(jnp.where(mine, pull, 0.0))
    values = moved_to + pulls
    left = lax.broadcasted_iota(jnp.int32, (16, LANES), 1) < 64
    for r in range(3):
        even, odd = values[2 * r], values[2 * r + 1]
        rest[0, r] = jnp.where(left, even, pltpu.roll(odd, 64, 1))
        rest[1, r] = jnp.where(left, pltpu.roll(even, 64, 1), odd)
        for tile in range(16):
            back[2 * tile, r] = rest[0, r, tile : tile + 1]
            back[2 * tile + 1, r] = rest[1, r, tile : tile + 1]


def third_kernel(
    edge, up, down, fluid, density, velocities, force, ys, zcat, state, out_up, out_down, post, weighted, spread
):
    weigh(weighted, ys, lambda axis, tile: force[axis, tile : tile + 1], state, OUTSIDE, INNER)
    spread[...] = contract(weighted[...], zcat[...])
    for p, x in enumerate(OUTSIDE):
        for tile in range(3):
            rows = slice(tile * 8, tile * 8 + 8)

            def put(i, value):
                post[i, p, rows] = value

            values = edge_values(edge, up, down, x, rows)
            velocity = [velocities[pl.ds((axis * 2 + p) * INNER + tile * 8, 8)] for axis in range(3)]
            is_fluid = fluid[x, rows]
            relaxed(values, density[p, rows], velocity, is_fluid > 0.5, put)
            pushed = spread_at(spread, p, tile, INNER, is_fluid)
            forced(lambda i: post[i, p, rows], pushed, put)
    for j, index in enumerate(UP):
        out_up[j] = moved(post[index, 1], index, HALO - TRIM)[0:ROWS]
    for j, index in enumerate(DOWN):
        out_down[j] = moved(post[index, 0], index, HALO - TRIM)[0:ROWS]


def stream_kernel(inside, outside, fluid, force, ys, zcat, state, out, post, weighted, spread):
    weigh(weighted, ys, lambda axis, tile: force[axis, tile : tile + 1], state, INSIDE, INNER)
    spread[...] = contract(weighted[...], zcat[...])
    for p, x in enumerate(INSIDE):
        for tile in range(3):
            rows = slice(tile * 8, tile * 8 + 8)

            def put(i, value):
                post[i, p, rows] = value

            forced(lambda i: inside[i, p, rows], spread_at(spread, p, tile, INNER, fluid[x, rows]), put)
    for index in range(19):
        for x in range(CX):
            source = x - DIRS[index][0]
            if 0 <= source < CX:
                plane = post[index, source - 1] if source in INSIDE else outside[index, source // 3]
                out[index, x] = moved(plane, index, HALO - TRIM)[0:ROWS]
            else:
                out[index, x] = jnp.zeros((ROWS, NZ), F32)


def fill_kernel(part, up, down, out, sems):
    copies = []
    for j, index in enumerate(UP):
        copies.append(pltpu.make_async_copy(up.at[j], out.at[index, 0], sems.at[j]))
    for j, index in enumerate(DOWN):
        copies.append(pltpu.make_async_copy(down.at[j], out.at[index, CX - 1], sems.at[5 + j]))
    for copy in copies:
        copy.start()
    for copy in copies:
        copy.wait()


def tail_kernel(back, moved_to, force):
    for r in range(3):
        total = functools.reduce(lambda a, b: a + b, [back[peer, r] for peer in range(back.shape[0])])
        for k, value in ((2 * r, total), (2 * r + 1, pltpu.roll(total, 64, 1))):
            target = moved_to if k < 3 else force
            target[k % 3 : k % 3 + 1] = value[:, 0:64]


IN_VMEM = pl.BlockSpec(memory_space=pltpu.VMEM)
ANYWHERE = pl.BlockSpec(memory_space=pl.ANY)


def near(x):
    return pltpu.with_memory_space_constraint(x, pltpu.VMEM)


def run(kernel, args, outs, scratch=(), cost=4_000_000):
    return pl.pallas_call(
        kernel,
        out_shape=outs,
        in_specs=[IN_VMEM] * len(args),
        out_specs=jax.tree.map(lambda _: IN_VMEM, outs, is_leaf=lambda leaf: not isinstance(leaf, tuple)),
        scratch_shapes=list(scratch),
        compiler_params=pltpu.CompilerParams(vmem_limit_bytes=24 * 2**20),
        cost_estimate=pl.CostEstimate(flops=0, transcendentals=0, bytes_accessed=cost),
    )(*args)


def ring(axis):
    peers = lax.axis_size(axis)
    forward = [(i, (i + 1) % peers) for i in range(peers)]
    return forward, [(j, i) for i, j in forward]


def parts(populations, solid, marker_corner, marker_frac, marker_target, stiffness, displacement):
    peers = lax.axis_size("sub")
    sub_up, sub_down = ring("sub")
    plate_up, plate_down = ring("plate")
    args = (populations, solid, marker_corner, marker_frac, marker_target, stiffness.reshape(1, 64), displacement)
    shape = (SENT_ROWS, NZ)
    sent, cells, bottom, top = pl.pallas_call(
        pack_kernel,
        out_shape=(
            jax.ShapeDtypeStruct((peers, 3, 2, LANES), F32),
            pltpu.VMEM((20, CX, ROWS, NZ), F32),
            pltpu.VMEM(shape, F32),
            pltpu.VMEM(shape, F32),
        ),
        in_specs=[pl.BlockSpec(memory_space=pltpu.HBM)] * 7,
        out_specs=[pl.BlockSpec(memory_space=pltpu.HBM), *[IN_VMEM] * 3],
        scratch_shapes=[
            pltpu.VMEM((8, LANES), F32),
            pltpu.VMEM(solid.shape, jnp.int32),
            pltpu.VMEM((peers, 3, 2, LANES), F32),
            *[pltpu.VMEM(arg.shape, arg.dtype) for arg in args[2:]],
            pltpu.SemaphoreType.DMA((8,)),
        ],
        compiler_params=pltpu.CompilerParams(vmem_limit_bytes=8 * 2**20),
        name="pack_kernel",
    )(*[pltpu.with_memory_space_constraint(arg, pltpu.HBM) for arg in args])
    markers = lax.all_to_all(sent, "sub", 0, 0, tiled=True)
    low = lax.ppermute(bottom, "sub", sub_up)
    high = lax.ppermute(top, "sub", sub_down)
    zcat, ys, given = run(
        weights_kernel,
        (near(markers),),
        (
            pltpu.VMEM((2 * NZ, MARKERS), BF16),
            pltpu.VMEM((EXT, MARKERS), F32),
            pltpu.VMEM((FORCE, 16, LANES), F32),
        ),
        (pltpu.VMEM((WORK, 16, LANES), F32),),
    )
    half = (pltpu.VMEM((3 * CX * ROWS, 2 * NZ), BF16), pltpu.VMEM((19, CX, ROWS, NZ), F32))
    vown, own, walls = run(own_kernel, (near(cells),), (*half, pltpu.VMEM((CX, ROWS, NZ), F32)))
    vouter, outer, fluid, fluid_inner = run(
        outer_kernel,
        (near(low), near(walls), near(high)),
        (*half, pltpu.VMEM((CX, EXT, NZ), F32), pltpu.VMEM((CX, INNER, NZ), F32)),
    )
    faces = (pltpu.VMEM((5, INNER, NZ), F32),) * 2
    plane_pairs = pltpu.VMEM((19, 2, INNER, NZ), F32)
    rows = pltpu.VMEM((3, 16, LANES), F32)

    def spreading(cells):
        return (pltpu.VMEM((12 * cells, MARKERS), BF16), pltpu.VMEM((12 * cells, 2 * NZ), F32))

    up, down, push, state = run(
        first_kernel,
        (near(vown), near(vouter), near(own), near(outer), near(fluid), near(zcat), near(ys), near(given)),
        (*faces, pltpu.VMEM((3, 2, EXT, NZ), F32), pltpu.VMEM((STATE, 16, LANES), F32)),
        (rows, *spreading(EXT)),
    )
    up = lax.ppermute(up, "plate", plate_up)
    down = lax.ppermute(down, "plate", plate_down)
    known = (near(ys), near(zcat), near(state))
    trimmed = pltpu.VMEM((INNER, MARKERS), F32)
    edge, found, inside, ys = run(
        inner_kernel,
        (near(own), near(outer), near(fluid), near(fluid_inner), near(push), *known),
        (plane_pairs, rows, pltpu.HBM((19, 2, INNER, NZ), F32), trimmed),
        (
            pltpu.VMEM((19, CX, EXT, NZ), F32),
            plane_pairs,
            pltpu.VMEM((6 * INNER, NZ), F32),
            *spreading(EXT),
        ),
        cost=12_000_000,
    )
    known = (near(ys), near(zcat), near(state))
    edges = (near(edge), near(up), near(down))
    force, density, velocities, back = run(
        second_kernel,
        (*edges, *known, near(found)),
        (
            rows,
            pltpu.VMEM((2, INNER, NZ), F32),
            pltpu.VMEM((6 * INNER, NZ), F32),
            jax.ShapeDtypeStruct((peers, 3, 1, LANES), F32),
        ),
        (rows, pltpu.VMEM((2, 3, 16, LANES), F32)),
    )
    back = lax.all_to_all(back, "sub", 0, 0, tiled=True)
    up, down, outside = run(
        third_kernel,
        (*edges, near(fluid_inner), near(density), near(velocities), near(force), *known),
        (*[pltpu.VMEM((5, ROWS, NZ), F32)] * 2, plane_pairs),
        spreading(INNER),
    )
    up = lax.ppermute(up, "plate", plate_up)
    down = lax.ppermute(down, "plate", plate_down)
    part = run(
        stream_kernel,
        (pltpu.with_memory_space_constraint(inside, pltpu.HBM), near(outside), near(fluid_inner), near(force), *known),
        jax.ShapeDtypeStruct((19, CX, ROWS, NZ), F32),
        (plane_pairs, *spreading(INNER)),
        cost=12_000_000,
    )
    out = pl.pallas_call(
        fill_kernel,
        out_shape=jax.ShapeDtypeStruct((19, CX, ROWS, NZ), F32),
        in_specs=[ANYWHERE, IN_VMEM, IN_VMEM],
        out_specs=ANYWHERE,
        scratch_shapes=[pltpu.SemaphoreType.DMA((10,))],
        input_output_aliases={0: 0},
        compiler_params=pltpu.CompilerParams(vmem_limit_bytes=8 * 2**20),
        name="fill_kernel",
    )(part, near(up), near(down))
    moved_to, force = run(tail_kernel, (near(back),), (jax.ShapeDtypeStruct((3, 64), F32),) * 2)
    return (out, moved_to, force)


def solution(mesh):
    in_specs = (
        P(None, "plate", "sub", None),
        P("plate", "sub", None),
        P(None, ("plate", "sub")),
        P(None, ("plate", "sub")),
        P(None, ("plate", "sub")),
        P(("plate", "sub")),
        P(None, ("plate", "sub")),
    )
    out_specs = (
        P(None, "plate", "sub", None),
        P(None, ("plate", "sub")),
        P(None, ("plate", "sub")),
    )
    return jax.shard_map(parts, mesh=mesh, in_specs=in_specs, out_specs=out_specs, check_vma=False)
```
